512 devices in a mesh: tile: 128 (over x, z, core), rep: 4 (over y).
Axes of the slice: x: 4, y: 4, z: 16, core: 2. Of those that a mesh axis runs over, the one named last changes fastest.
Arguments:
- embedding: bfloat16 [2048, 64, 256], P('tile'), may hold values from -6 to 6
- prompt_tile: int32 [65536, 1], P(('tile', 'rep')), may hold values from 0 to 127; in each aligned block of 128 rows (0 to 127, 128 to 255, ...) at most 2 rows name the same one
- crop_row: int32 [65536], P(('tile', 'rep')), may hold values from 0 to 15
- crop_col: int32 [65536], P(('tile', 'rep')), may hold values from 0 to 60
- points: int32 [65536, 2], P(('tile', 'rep')), may hold values from 0 to 15
- confidence: int32 [65536], P(('tile', 'rep')), may hold values from 1 to 4
- pe_matrix: float32 [2, 128], replicated, may hold values from -5 to 5
- point_embed: float32 [256], replicated, may hold values from -5 to 5
- w_one: bfloat16 [256, 256], replicated, may hold values from -0.375 to 0.375
- w_two: bfloat16 [256, 256], replicated, may hold values from -0.375 to 0.375
- w_three: bfloat16 [256, 32], replicated, may hold values from -0.375 to 0.375
- conv_one: bfloat16 [256, 256], replicated, may hold values from -0.375 to 0.375
- conv_two: bfloat16 [64, 128], replicated, may hold values from -0.75 to 0.75
Outputs:
- mask_sum: float32 [8192, 256], P('tile')
The draws below stay inside these ranges and needn't reach their ends.
Inputs may be any that keep to these rules, and one draw needn't show every extreme that they name: `prompt_tile`: among the prompts of one device no strip is named more than 2 times, and some device names some strip exactly 2 times.
All inputs are finite; a program needn't handle non-finite values.
Results may differ from the reference program's by a relative error of at most 0.0049.
Values may be sent and summed in bfloat16 or wider, within the bound.
No kernel may reach another device: no remote copies, remote signals or barrier semaphores. Data moves between devices by JAX's collectives and lax.ppermute only.
A program may use at most 64 MiB of HBM per device.

```python
import math
import jax
import jax.numpy as jnp
import numpy as np
from jax import lax

C = 256
C1 = 64
C2 = 32
HID = 256
CK = 4
ROWS_T = 16
EW = 64
P_DEV = 128
MOST = 2
PROMPTS = 65536
EH = 2048
N_TILE = 128


def set_ends(array, rng, smallest, top_value):
    place = [jax.random.randint(jax.random.fold_in(rng, axis), (), 0, length) for axis, length in enumerate(array.shape)]
    longest = array.shape.index(max(array.shape))
    next_to = place[:longest] + [(place[longest] + 1) % array.shape[longest]] + place[longest + 1:]
    return array.at[tuple(place)].set(smallest).at[tuple(next_to)].set(top_value)


def levels(stream_key, extent, shards, low, largest):
    level = 1.0
    for position, parts in shards:
        draws = jax.random.uniform(jax.random.fold_in(jax.random.fold_in(stream_key, 6), position), (parts,), jnp.float32, low / len(shards), largest / len(shards))
        level = level * jnp.repeat(jnp.exp(draws), extent[position] // parts).reshape((-1,) + (1,) * (len(extent) - 1 - position))
    return level


def routed_block(key, own, number, rows, number_of, top, most, slope):
    sequence = jax.random.permutation(key, number_of)
    heavy_load, common = portions_of(number_of, rows * top, most, slope, True), portions_of(number_of, rows * top, most, slope, False)
    places = jnp.arange(number_of)

    def named(tallies, turn):
        used = int((tallies > 0).sum())
        fixed = max(1, used // 4)
        passed = fixed + (places - fixed + turn * (used - fixed)) % max(1, number_of - fixed)
        return jnp.zeros((number_of,), jnp.int32).at[sequence[jnp.where(places < fixed, places, passed)]].set(jnp.asarray(tallies, jnp.int32))

    tallies = jnp.where(number % 4 == 0, named(heavy_load, number // 4), named(common, number - number // 4 - 1))
    mixed = jax.random.permutation(jax.random.fold_in(own, 3), number_of)
    donor, taker = mixed[0:number_of // 2 * 2:2], mixed[1:number_of // 2 * 2:2]
    slack = jnp.minimum(tallies[donor] - 1, most - tallies[taker]) // 2
    slack = jnp.where((donor == sequence[0]) | (taker == sequence[0]) | (tallies[taker] == 0), 0, jnp.maximum(slack, 0))
    passed = jax.random.randint(jax.random.fold_in(own, 4), (number_of // 2,), 0, 1 << 20) % (slack + 1)
    tallies = tallies.at[donor].add(-passed).at[taker].add(passed)
    labels = jnp.searchsorted(jnp.cumsum(tallies), jnp.arange(rows * top), side="right").astype(jnp.int32)
    grid = labels.reshape(top, rows).T
    grid = grid[jax.random.permutation(jax.random.fold_in(own, 1), rows)]
    turn = jax.random.randint(jax.random.fold_in(own, 2), (rows, 1), 0, top)
    return jnp.take_along_axis(grid, (jnp.arange(top)[None, :] + turn) % top, axis=1)


def portions_of(count, total, bound, lean, full):
    loads = [(1 << 20) // math.isqrt(standing ** lean) + 1 for standing in range(1, count + 1)]
    largest = bound if full else min(bound, max(-(-total // count), total * loads[0] // sum(loads)))
    least = 1 if total - largest >= count - 1 else 0
    holding, surplus = [largest] + [least] * (count - 1), total - largest - least * (count - 1)
    while surplus > 0:
        free = [i for i in range(1, count) if holding[i] < largest] or [i for i in range(1, count) if holding[i] < bound]
        pool, remaining = sum([loads[i] for i in free]), surplus
        for i in free:
            addition = min(bound - holding[i], max(1, remaining * loads[i] // pool), surplus)
            holding[i] = holding[i] + addition
            surplus = surplus - addition
    return np.array(holding)


def noise(own_key, dims, width, reach, cuts=(), held_as=jnp.bfloat16):
    values = width * jax.random.normal(own_key, dims, jnp.float32)
    if cuts:
        values = values * levels(own_key, dims, cuts, -0.22, 0.18)
    return jnp.clip(values, -reach, reach).astype(held_as)


def setup_inputs(seed: int = 0) -> dict:
    splits = jax.random.split(jax.random.key(seed), 14)
    embedding = noise(splits[0], (EH, EW, C), 1.0, 6.0, ((0, 128),))
    prompt_tile_keys = jax.random.split(jax.random.fold_in(splits[1], 1), PROMPTS // P_DEV)
    prompt_tile_turns = jax.random.permutation(jax.random.fold_in(splits[1], 3), PROMPTS // P_DEV)
    prompt_tile = jax.vmap(lambda own, number: routed_block(jax.random.fold_in(splits[1], 2), own, number, P_DEV, N_TILE, 1, MOST, 2))(prompt_tile_keys, prompt_tile_turns).reshape((PROMPTS, 1))
    crop_row = set_ends(jax.random.randint(splits[2], (PROMPTS,), 0, ROWS_T), jax.random.fold_in(splits[2], 1), 0, ROWS_T - 1).astype(jnp.int32)
    crop_col = set_ends(jax.random.randint(splits[3], (PROMPTS,), 0, EW - CK + 1), jax.random.fold_in(splits[3], 1), 0, EW - CK).astype(jnp.int32)
    points = set_ends(jax.random.randint(splits[4], (PROMPTS, 2), 0, 4 * CK), jax.random.fold_in(splits[4], 1), 0, (4 * CK) - 1).astype(jnp.int32)
    confidence = set_ends(jax.random.randint(splits[5], (PROMPTS,), 1, 5), jax.random.fold_in(splits[5], 1), 1, 4).astype(jnp.int32)
    pe_matrix = noise(splits[6], (2, C // 2), 1.0, 5.0, (), jnp.float32)
    point_embed = noise(splits[7], (C,), 1.0, 5.0, (), jnp.float32)
    w_one = noise(splits[8], (C, HID), C ** -0.5, 0.375)
    w_two = noise(splits[9], (HID, HID), HID ** -0.5, 0.375)
    w_three = noise(splits[10], (HID, C2), HID ** -0.5, 0.375)
    conv_one = noise(splits[11], (C, 4 * C1), C ** -0.5, 0.375)
    conv_two = noise(splits[12], (C1, 4 * C2), C1 ** -0.5, 0.75)
    return dict(embedding=embedding, prompt_tile=prompt_tile, crop_row=crop_row, crop_col=crop_col, points=points, confidence=confidence, pe_matrix=pe_matrix, point_embed=point_embed, w_one=w_one, w_two=w_two, w_three=w_three, conv_one=conv_one, conv_two=conv_two)


def prompt_heads(points, pe_matrix, point_embed, w_one, w_two, w_three):
    coords = (points.astype(jnp.float32) + 0.5) / (4.0 * CK) * 2.0 - 1.0
    angles = (coords[:, 0:1] * pe_matrix[0][None, :] + coords[:, 1:2] * pe_matrix[1][None, :]) * (2.0 * math.pi)
    tokens = (jnp.concatenate([jnp.sin(angles), jnp.cos(angles)], axis=1) + point_embed[None, :]).astype(jnp.bfloat16)
    hidden_one = jax.nn.relu(jnp.dot(tokens, w_one, preferred_element_type=jnp.float32)).astype(jnp.bfloat16)
    hidden_two = jax.nn.relu(jnp.dot(hidden_one, w_two, preferred_element_type=jnp.float32)).astype(jnp.bfloat16)
    return jnp.dot(hidden_two, w_three, preferred_element_type=jnp.float32).astype(jnp.bfloat16)

def mask_terms(crop_cells, head_rows, scale_rows, conv_one, conv_two):
    amount, crop_side, channels = (crop_cells.shape[0], crop_cells.shape[1], crop_cells.shape[3])
    mid_width = conv_one.shape[1] // 4
    narrow = conv_two.shape[1] // 4
    first_up = jnp.dot(crop_cells.reshape(amount * crop_side * crop_side, channels), conv_one, preferred_element_type=jnp.float32)
    first_up = first_up.reshape(amount * crop_side * crop_side * 4, mid_width)
    centre = first_up - lax.optimization_barrier(jnp.mean(first_up, axis=1, keepdims=True))
    normed = centre * lax.rsqrt(lax.optimization_barrier(jnp.mean(centre * centre, axis=1, keepdims=True)) + 1e-06)
    active = jax.nn.gelu(normed, approximate=False).astype(jnp.bfloat16)
    second = jnp.dot(active, conv_two, preferred_element_type=jnp.float32)
    upscaled = jax.nn.gelu(second, approximate=False).astype(jnp.bfloat16).reshape(amount, crop_side * crop_side * 16, narrow)
    logits = jnp.einsum('nqc,nc->nq', upscaled.astype(jnp.float32), head_rows.astype(jnp.float32))
    logits = logits.reshape(amount, crop_side, crop_side, 2, 2, 2, 2).transpose(0, 1, 3, 5, 2, 4, 6)
    logits = logits.reshape(amount, 4 * crop_side, 4 * crop_side)
    return (logits * scale_rows[:, None, None]).astype(jnp.bfloat16)

def reference(embedding, prompt_tile, crop_row, crop_col, points, confidence, pe_matrix, point_embed, w_one, w_two, w_three, conv_one, conv_two):
    dynamic_heads = prompt_heads(points, pe_matrix, point_embed, w_one, w_two, w_three)
    top_rows = (prompt_tile[:, 0] * ROWS_T + crop_row).astype(jnp.int32)
    left_cols = crop_col.astype(jnp.int32)
    scales = confidence.astype(jnp.float32) / 4.0
    padded = jnp.concatenate([embedding, jnp.zeros((CK - 1, EW, C), jnp.bfloat16)], axis=0)
    blocks = PROMPTS // 64

    def block_terms(group_in):
        row_group, col_group, head_group, scale_group = group_in
        crop_cells = jax.vmap(lambda row_at, col_at: lax.dynamic_slice(padded, (row_at, col_at, jnp.int32(0)), (CK, CK, C)))(row_group, col_group)
        return mask_terms(crop_cells, head_group, scale_group, conv_one, conv_two)
    mask_patches = lax.map(block_terms, (top_rows.reshape(blocks, 64), left_cols.reshape(blocks, 64), dynamic_heads.reshape(blocks, 64, C2), scales.reshape(blocks, 64)))
    mask_patches = mask_patches.reshape(PROMPTS, 4 * CK, 4 * CK)
    canvas = jnp.zeros((4 * EH + 4 * CK - 4, 4 * EW), jnp.float32)

    def place_one(canvas, scan_item):
        patch_in, row_at, col_at = scan_item
        start_row = (4 * row_at).astype(jnp.int32)
        start_col = (4 * col_at).astype(jnp.int32)
        current = lax.dynamic_slice(canvas, (start_row, start_col), (4 * CK, 4 * CK))
        return (lax.dynamic_update_slice(canvas, current + patch_in.astype(jnp.float32), (start_row, start_col)), None)
    canvas, unused = lax.scan(place_one, canvas, (mask_patches, top_rows, left_cols))
    return canvas[:4 * EH]
```

```python
import math

import jax
import jax.numpy as jnp
from jax import lax
from jax.experimental import pallas as pl
from jax.experimental.pallas import tpu as pltpu
from jax.sharding import Mesh
from jax.sharding import PartitionSpec as P

CK = 4
C = 256
C1 = 64
C2 = 32
ROWS_T = 16
EW = 64
P_DEV = 128
NX, NZ, NC, NR = 4, 16, 2, 4
CELLS = ROWS_T * EW
F32 = jnp.float32
BF16 = jnp.bfloat16
I32 = jnp.int32


def iota(shape, dim):
    return lax.broadcasted_iota(I32, shape, dim)


def nt(a, b):
    return lax.dot_general(a, b, (((1,), (1,)), ((), ())), preferred_element_type=F32)


def nn(a, b):
    return jnp.dot(a, b, preferred_element_type=F32)


def gelu(v):
    return 0.5 * v * (1.0 + lax.erf(v * (1.0 / math.sqrt(2.0))))


def local_tables(emb, one, two, pe, bias, w1, w2, w3, up_ref, head_ref):
    q = iota((256, P_DEV), 0)
    first = ((q >> 4).astype(F32) + 0.5) / (4.0 * CK) * 2.0 - 1.0
    second = ((q & 15).astype(F32) + 0.5) / (4.0 * CK) * 2.0 - 1.0
    pe_value = pe[...]
    angles = (first * pe_value[0:1, :] + second * pe_value[1:2, :]) * (2.0 * math.pi)
    tokens = (jnp.concatenate([jnp.sin(angles), jnp.cos(angles)], axis=1) + bias[...]).astype(BF16)
    hidden = jnp.maximum(nn(tokens, w1[...]), 0.0).astype(BF16)
    hidden = jnp.maximum(nn(hidden, w2[...]), 0.0).astype(BF16)
    head_ref[...] = nn(hidden, w3[...]).astype(BF16)

    row = iota((512, P_DEV), 0)
    k, x, y = row >> 4, (row >> 2) & 3, row & 3
    pick = (iota((512, P_DEV), 1) == (2 * (y & 1) + (x & 1)) * C2 + k).astype(BF16)
    row = iota((512, 256), 0)
    off = 2 * ((row & 3) >> 1) + (((row >> 2) & 3) >> 1)
    keep = (iota((512, 256), 1) >> 6) == off
    two_tiled = jnp.concatenate([two[...]] * 4, axis=0)
    wide = jnp.where(keep, nt(pick, two_tiled), 0.0).astype(BF16)
    one_t = one[...].astype(F32).T.astype(BF16)

    def block(i, carry):
        start = pl.multiple_of(i * 128, 128)
        first_up = nt(one_t, emb[pl.ds(start, 128), :])
        parts = []
        for o in range(4):
            v = first_up[o * C1 : (o + 1) * C1, :]
            v = v - jnp.mean(v, axis=0, keepdims=True)
            v = v * lax.rsqrt(jnp.mean(v * v, axis=0, keepdims=True) + 1e-06)
            parts.append(gelu(v).astype(BF16))
        active = jnp.concatenate(parts, axis=0)
        up_ref[:, pl.ds(start, 128)] = gelu(nn(wide, active)).astype(BF16)
        return carry

    lax.fori_loop(0, CELLS // 128, block, 0)


def gathered_in(refs, bufs, sems):
    copies = [pltpu.make_async_copy(r, b, sems.at[i]) for i, (r, b) in enumerate(zip(refs, bufs))]
    for c in copies:
        c.start()
    for c in copies:
        c.wait()


def store_out(up_buf, head_buf, up_ref, head_ref, sems):
    copies = [
        pltpu.make_async_copy(up_buf, up_ref, sems.at[0]),
        pltpu.make_async_copy(head_buf, head_ref, sems.at[1]),
    ]
    for c in copies:
        c.start()
    for c in copies:
        c.wait()


def is_early():
    z = lax.axis_index("z")
    return (z <= 4) | (z >= 12)


def slots_kernel(early, tile, row, col, pts, conf, *rest):
    weights, (send, up, head), scratch = rest[:8], rest[8:11], rest[11:]
    bufs, (up_buf, head_buf, sems) = scratch[:8], scratch[8:]
    t = tile[...]
    names = (iota((P_DEV, P_DEV), 0) == t).astype(F32)
    before = (iota((P_DEV, P_DEV), 0) < iota((P_DEV, P_DEV), 1)).astype(BF16)
    count = nn(names.astype(BF16), before)
    rank = jnp.sum(names * count, axis=0, keepdims=True).astype(I32)
    values = [row[...], col[...], conf[...], pts[0:1, :], pts[1:2, :]]
    group = iota((16, P_DEV), 0)
    x_of, s_of = group >> 2, group & 3
    dest = iota((NZ * NC, P_DEV), 0)

    def part(target, rank_at, values):
        mask = ((target >> 5) == x_of) & (rank_at == s_of)
        rows = [jnp.where(mask, v.astype(F32), 0.0) for v in values]
        rows += [jnp.zeros((16, P_DEV), F32)] * 3
        return nt(
            ((target & 31) == dest).astype(BF16), jnp.concatenate(rows, axis=0).astype(BF16)
        )

    out = part(t, rank, values) + part(t + 1, rank + 2, [values[0] - ROWS_T] + values[1:])
    send[...] = out.reshape(NZ * NC, 1, 128)

    @pl.when(early[0] == 1)
    def _():
        gathered_in(weights, bufs, sems)
        local_tables(*bufs, up_buf, head_buf)
        store_out(up_buf, head_buf, up, head, sems)


def late_kernel(early, up_in, head_in, *rest):
    weights, (up, head), scratch = rest[:8], rest[8:10], rest[10:]
    bufs, (up_buf, head_buf, sems) = scratch[:8], scratch[8:]

    @pl.when(early[0] != 1)
    def _():
        gathered_in(weights, bufs, sems)
        local_tables(*bufs, up_buf, head_buf)
        store_out(up_buf, head_buf, up, head, sems)


def regroup_kernel(got, send):
    r = got[...].reshape(NZ * NC, 128)
    r = jnp.concatenate([r] * 4, axis=0)
    keep = (iota((128, 128), 1) & 3) == (iota((128, 128), 0) >> 5)
    r = jnp.where(keep, r, 0.0).astype(BF16)
    at, lane = iota((32, 128), 0), iota((32, 128), 1)
    pick = ((lane >> 4) == (at & 7)) & (((lane >> 2) & 3) == (at >> 3))
    out = nt(pick.astype(BF16), r)
    for x in range(NX):
        for y in range(NR):
            send[x * NR + y] = out[x * 8 : (x + 1) * 8, :].astype(BF16)


def mask_kernel(got, up, head, out):
    lane = iota((8, 128), 1)
    own, below = [], []
    for j in range(8):
        a, b = got[j].astype(F32), got[j + 8].astype(F32)
        own.append(jnp.where(lane < 64, a, pltpu.roll(b, 64, 1)))
        below.append(jnp.where(lane < 64, pltpu.roll(a, 64, 1), b))
    own, below = jnp.concatenate(own, axis=1), jnp.concatenate(below, axis=1)
    many = 1024
    r_at = iota((16, many), 0).astype(F32)
    c_at = iota((EW, many), 0).astype(F32)
    table = head[...]

    def one_hot(v, at):
        return (at == v).astype(BF16)

    def factors(v, rows):
        row, col, conf, first, second = (v[i : i + 1, :] for i in range(5))
        hot_a, hot_b = one_hot(first, r_at), one_hot(second, r_at)
        hot = jnp.concatenate([hot_a[i : i + 1, :] * hot_b for i in range(16)], axis=0)
        heads = lax.dot_general(table, hot, (((0,), (0,)), ((), ())), preferred_element_type=F32)
        heads = heads.astype(BF16)
        d = r_at - row
        in_row = ((d >= 0.0) & (d <= 3.0)).astype(BF16)
        d = c_at - col
        in_col = jnp.where((d >= 0.0) & (d <= 3.0), conf, 0.0).astype(BF16)
        blank = jnp.zeros((EW, many), BF16)
        even, odd = jnp.concatenate([in_col, blank], axis=0), jnp.concatenate([blank, in_col], axis=0)
        lefts = [heads * in_row[i : i + 1, :] for i in range(rows)]
        return (
            nt(jnp.concatenate(lefts[0::2], axis=0), even)
            + nt(jnp.concatenate(lefts[1::2], axis=0), odd)
        )

    total = factors(own, 16)
    spill = factors(below, 4)
    total = jnp.concatenate([total[:64] + spill, total[64:]], axis=0)

    sub = iota((8, 128), 0)
    mine = (sub >> 2) == (iota((8, 128), 1) >> 6)
    blocks = []
    for j in range(8):
        h = total[j * 32 : (j + 1) * 32, :]
        low, high = jnp.zeros((8, 128), F32), jnp.zeros((8, 128), F32)
        for k in range(C2):
            u = up[k * 16 : (k + 1) * 16, j * 128 : (j + 1) * 128].astype(F32)
            w = h[k : k + 1, :]
            low, high = low + u[:8] * w, high + u[8:] * w
        pieces = []
        for v in (low, high):
            turned = pltpu.roll(v, 4, 0)
            pieces.append(jnp.where(mine, jnp.where(sub < 4, v, turned), 0.0))
            pieces.append(jnp.where(mine, jnp.where(sub < 4, turned, v), 0.0))
        blocks.append(jnp.concatenate(pieces, axis=1))
    flat = jnp.concatenate(blocks, axis=0) * 0.25
    at, lane = iota((512, 256), 0), iota((512, 256), 1)
    spread = (lane == 4 * (at & 63) + (at >> 7)).astype(BF16)
    top = flat.astype(BF16)
    rest = flat - top.astype(F32)
    mid = rest.astype(BF16)
    last = (rest - mid.astype(F32)).astype(BF16)
    out[...] = nn(top, spread) + (nn(mid, spread) + nn(last, spread))


def on_device(
    embedding,
    prompt_tile,
    crop_row,
    crop_col,
    points,
    confidence,
    pe_matrix,
    point_embed,
    w_one,
    w_two,
    w_three,
    conv_one,
    conv_two,
):
    early = is_early().astype(I32).reshape(1)
    smem = pl.BlockSpec(memory_space=pltpu.SMEM)
    vmem = pl.BlockSpec(memory_space=pltpu.VMEM)
    hbm = pl.BlockSpec(memory_space=pl.ANY)
    weights = (
        embedding.reshape(CELLS, C),
        conv_one,
        conv_two,
        pe_matrix,
        point_embed.reshape(1, 256),
        w_one,
        w_two,
        w_three,
    )
    up_shape = jax.ShapeDtypeStruct((16 * C2, CELLS), BF16)
    head_shape = jax.ShapeDtypeStruct((256, C2), BF16)
    scratch = [pltpu.VMEM(w.shape, w.dtype) for w in weights] + [
        pltpu.VMEM(up_shape.shape, BF16),
        pltpu.VMEM(head_shape.shape, BF16),
        pltpu.SemaphoreType.DMA((8,)),
    ]
    send, up, head = pl.pallas_call(
        slots_kernel,
        out_shape=(jax.ShapeDtypeStruct((NZ * NC, 1, 128), F32), up_shape, head_shape),
        in_specs=[smem] + [vmem] * 5 + [hbm] * 8,
        out_specs=(vmem, hbm, hbm),
        scratch_shapes=scratch,
    )(
        early,
        prompt_tile.reshape(1, P_DEV),
        crop_row.reshape(1, P_DEV),
        crop_col.reshape(1, P_DEV),
        points.T,
        confidence.reshape(1, P_DEV),
        *weights,
    )
    got = lax.all_to_all(send, ("z", "core"), 0, 0, tiled=True)
    up, head = pl.pallas_call(
        late_kernel,
        out_shape=(up_shape, head_shape),
        in_specs=[smem] + [hbm] * 10,
        out_specs=(hbm, hbm),
        scratch_shapes=scratch,
        input_output_aliases={1: 0, 2: 1},
    )(early, up, head, *weights)
    send = pl.pallas_call(
        regroup_kernel,
        out_shape=jax.ShapeDtypeStruct((NX * NR, 8, 128), BF16),
        in_specs=[vmem],
        out_specs=vmem,
    )(got)
    got = lax.all_to_all(send, ("x", "rep"), 0, 0, tiled=True)
    return pl.pallas_call(
        mask_kernel,
        out_shape=jax.ShapeDtypeStruct((4 * ROWS_T, 4 * EW), F32),
        in_specs=[vmem] * 3,
        out_specs=vmem,
    )(got, up, head)


def solution(mesh):
    split = Mesh(mesh.devices.reshape(NX, NZ, NC, NR), ("x", "z", "core", "rep"))
    tile, every = ("x", "z", "core"), ("x", "z", "core", "rep")
    return jax.shard_map(
        on_device,
        mesh=split,
        in_specs=(
            P(tile, None, None),
            P(every, None),
            P(every),
            P(every),
            P(every, None),
            P(every),
            P(),
            P(),
            P(),
            P(),
            P(),
            P(),
            P(),
        ),
        out_specs=P(tile, None),
        check_vma=False,
    )
```

```python
import math

import jax
import jax.numpy as jnp
from jax import lax
from jax.experimental import pallas as pl
from jax.experimental.pallas import tpu as pltpu
from jax.sharding import Mesh
from jax.sharding import PartitionSpec as P

CK = 4
C = 256
C1 = 64
C2 = 32
ROWS_T = 16
EW = 64
P_DEV = 128
NX, NZ, NC, NR = 4, 16, 2, 4
CELLS = ROWS_T * EW
F32 = jnp.float32
BF16 = jnp.bfloat16
I32 = jnp.int32


def iota(shape, dim):
    return lax.broadcasted_iota(I32, shape, dim)


def nt(a, b):
    return lax.dot_general(a, b, (((1,), (1,)), ((), ())), preferred_element_type=F32)


def nn(a, b):
    return jnp.dot(a, b, preferred_element_type=F32)


def gelu(v):
    return 0.5 * v * (1.0 + lax.erf(v * (1.0 / math.sqrt(2.0))))


def local_tables(emb, one, two, pe, bias, w1, w2, w3, up_ref, head_ref):
    q = iota((256, P_DEV), 0)
    first = ((q >> 4).astype(F32) + 0.5) / (4.0 * CK) * 2.0 - 1.0
    second = ((q & 15).astype(F32) + 0.5) / (4.0 * CK) * 2.0 - 1.0
    pe_value = pe[...]
    angles = (first * pe_value[0:1, :] + second * pe_value[1:2, :]) * (2.0 * math.pi)
    tokens = (jnp.concatenate([jnp.sin(angles), jnp.cos(angles)], axis=1) + bias[...]).astype(BF16)
    hidden = jnp.maximum(nn(tokens, w1[...]), 0.0).astype(BF16)
    hidden = jnp.maximum(nn(hidden, w2[...]), 0.0).astype(BF16)
    head_ref[...] = nt(w3[...], hidden).astype(BF16)

    row = iota((512, P_DEV), 0)
    k, x, y = row >> 4, (row >> 2) & 3, row & 3
    pick = (iota((512, P_DEV), 1) == (2 * (y & 1) + (x & 1)) * C2 + k).astype(BF16)
    row = iota((512, 256), 0)
    off = 2 * ((row & 3) >> 1) + (((row >> 2) & 3) >> 1)
    keep = (iota((512, 256), 1) >> 6) == off
    two_tiled = jnp.concatenate([two[...]] * 4, axis=0)
    wide = jnp.where(keep, nt(pick, two_tiled), 0.0).astype(BF16)
    one_t = one[...].astype(F32).T.astype(BF16)

    def block(i, carry):
        start = pl.multiple_of(i * 128, 128)
        first_up = nt(one_t, emb[pl.ds(start, 128), :])
        parts = []
        for o in range(4):
            v = first_up[o * C1 : (o + 1) * C1, :]
            v = v - jnp.mean(v, axis=0, keepdims=True)
            v = v * lax.rsqrt(jnp.mean(v * v, axis=0, keepdims=True) + 1e-06)
            parts.append(gelu(v).astype(BF16))
        active = jnp.concatenate(parts, axis=0)
        up_ref[:, pl.ds(start, 128)] = gelu(nn(wide, active)).astype(BF16)
        return carry

    lax.fori_loop(0, CELLS // 128, block, 0)


def gathered_in(refs, bufs, sems):
    copies = [pltpu.make_async_copy(r, b, sems.at[i]) for i, (r, b) in enumerate(zip(refs, bufs))]
    for c in copies:
        c.start()
    for c in copies:
        c.wait()


def in_vmem(value):
    return pltpu.with_memory_space_constraint(value, pltpu.VMEM)


def is_early():
    return lax.axis_index("z") <= 3


def slots_kernel(early, tile, row, col, pts, conf, *rest):
    weights, (send, up, head), scratch = rest[:8], rest[8:11], rest[11:]
    bufs, sems = scratch[:8], scratch[8]
    t = tile[...]
    names = (iota((P_DEV, P_DEV), 0) == t).astype(F32)
    before = (iota((P_DEV, P_DEV), 0) < iota((P_DEV, P_DEV), 1)).astype(BF16)
    count = nn(names.astype(BF16), before)
    rank = jnp.sum(names * count, axis=0, keepdims=True).astype(I32)
    values = [row[...], col[...], conf[...], pts[0:1, :], pts[1:2, :]]
    group = iota((16, P_DEV), 0)
    x_of, s_of = group >> 2, group & 3
    dest = iota((NZ * NC, P_DEV), 0)

    def part(target, rank_at, values):
        mask = ((target >> 5) == x_of) & (rank_at == s_of)
        rows = [jnp.where(mask, v.astype(F32), 0.0) for v in values]
        rows += [jnp.zeros((16, P_DEV), F32)] * 3
        return nt(
            ((target & 31) == dest).astype(BF16), jnp.concatenate(rows, axis=0).astype(BF16)
        )

    out = part(t, rank, values) + part(t + 1, rank + 2, [values[0] - ROWS_T] + values[1:])
    send[...] = out.reshape(NZ * NC, 1, 128)

    @pl.when(early[0] == 1)
    def _():
        gathered_in(weights, bufs, sems)
        local_tables(*bufs, up, head)


def late_kernel(early, up_in, head_in, *rest):
    weights, (up, head), scratch = rest[:8], rest[8:10], rest[10:]
    bufs, sems = scratch[:8], scratch[8]

    @pl.when(early[0] != 1)
    def _():
        gathered_in(weights, bufs, sems)
        local_tables(*bufs, up, head)


def regroup_kernel(got, send):
    r = got[...].reshape(NZ * NC, 128)
    r = jnp.concatenate([r] * 4, axis=0)
    keep = (iota((128, 128), 1) & 3) == (iota((128, 128), 0) >> 5)
    r = jnp.where(keep, r, 0.0).astype(BF16)
    at, lane = iota((32, 128), 0), iota((32, 128), 1)
    pick = ((lane >> 4) == (at & 7)) & (((lane >> 2) & 3) == (at >> 3))
    out = nt(pick.astype(BF16), r)
    for x in range(NX):
        for y in range(NR):
            send[x * NR + y] = out[x * 8 : (x + 1) * 8, :].astype(BF16)


def mask_kernel(got, up, head, out):
    lane = iota((8, 128), 1)
    own, below = [], []
    for j in range(8):
        a, b = got[j].astype(F32), got[j + 8].astype(F32)
        own.append(jnp.where(lane < 64, a, pltpu.roll(b, 64, 1)))
        below.append(jnp.where(lane < 64, pltpu.roll(a, 64, 1), b))
    own, below = jnp.concatenate(own, axis=1), jnp.concatenate(below, axis=1)
    many = 1024
    r_at = iota((16, many), 0).astype(F32)
    c_at = iota((EW, many), 0).astype(F32)
    table = head[...]

    def one_hot(v, at):
        return (at == v).astype(BF16)

    def factors(v, rows):
        row, col, conf, first, second = (v[i : i + 1, :] for i in range(5))
        hot_a, hot_b = one_hot(first, r_at), one_hot(second, r_at)
        hot = jnp.concatenate([hot_a[i : i + 1, :] * hot_b for i in range(16)], axis=0)
        heads = nn(table, hot).astype(BF16)
        d = r_at - row
        in_row = ((d >= 0.0) & (d <= 3.0)).astype(BF16)
        d = c_at - col
        in_col = jnp.where((d >= 0.0) & (d <= 3.0), conf, 0.0).astype(BF16)
        blank = jnp.zeros((EW, many), BF16)
        even, odd = jnp.concatenate([in_col, blank], axis=0), jnp.concatenate([blank, in_col], axis=0)
        lefts = [heads * in_row[i : i + 1, :] for i in range(rows)]
        return (
            nt(jnp.concatenate(lefts[0::2], axis=0), even)
            + nt(jnp.concatenate(lefts[1::2], axis=0), odd)
        )

    total = factors(own, 16)
    spill = factors(below, 4)
    total = jnp.concatenate([total[:64] + spill, total[64:]], axis=0)

    sub = iota((8, 128), 0)
    mine = (sub >> 2) == (iota((8, 128), 1) >> 6)
    blocks = []
    for j in range(8):
        h = total[j * 32 : (j + 1) * 32, :]
        low, high = jnp.zeros((8, 128), F32), jnp.zeros((8, 128), F32)
        for k in range(C2):
            u = up[k * 16 : (k + 1) * 16, j * 128 : (j + 1) * 128].astype(F32)
            w = h[k : k + 1, :]
            low, high = low + u[:8] * w, high + u[8:] * w
        pieces = []
        for v in (low, high):
            turned = pltpu.roll(v, 4, 0)
            pieces.append(jnp.where(mine, jnp.where(sub < 4, v, turned), 0.0))
            pieces.append(jnp.where(mine, jnp.where(sub < 4, turned, v), 0.0))
        blocks.append(jnp.concatenate(pieces, axis=1))
    flat = jnp.concatenate(blocks, axis=0) * 0.25
    at, lane = iota((512, 256), 0), iota((512, 256), 1)
    spread = (lane == 4 * (at & 63) + (at >> 7)).astype(BF16)
    top = flat.astype(BF16)
    rest = flat - top.astype(F32)
    mid = rest.astype(BF16)
    last = (rest - mid.astype(F32)).astype(BF16)
    out[...] = nn(top, spread) + (nn(mid, spread) + nn(last, spread))


def on_device(
    embedding,
    prompt_tile,
    crop_row,
    crop_col,
    points,
    confidence,
    pe_matrix,
    point_embed,
    w_one,
    w_two,
    w_three,
    conv_one,
    conv_two,
):
    early = is_early().astype(I32).reshape(1)
    smem = pl.BlockSpec(memory_space=pltpu.SMEM)
    vmem = pl.BlockSpec(memory_space=pltpu.VMEM)
    hbm = pl.BlockSpec(memory_space=pl.ANY)
    weights = (
        embedding.reshape(CELLS, C),
        conv_one,
        conv_two,
        pe_matrix,
        point_embed.reshape(1, 256),
        w_one,
        w_two,
        w_three.T,
    )
    up_shape = pltpu.VMEM((16 * C2, CELLS), BF16)
    head_shape = pltpu.VMEM((C2, 256), BF16)
    scratch = [pltpu.VMEM(w.shape, w.dtype) for w in weights] + [pltpu.SemaphoreType.DMA((8,))]
    send, up, head = pl.pallas_call(
        slots_kernel,
        out_shape=(pltpu.VMEM((NZ * NC, 1, 128), F32), up_shape, head_shape),
        in_specs=[smem] + [vmem] * 5 + [hbm] * 8,
        out_specs=(vmem, vmem, vmem),
        scratch_shapes=scratch,
    )(
        early,
        prompt_tile.reshape(1, P_DEV),
        crop_row.reshape(1, P_DEV),
        crop_col.reshape(1, P_DEV),
        points.T,
        confidence.reshape(1, P_DEV),
        *weights,
    )
    got = lax.all_to_all(send, ("z", "core"), 0, 0, tiled=True)
    up, head = pl.pallas_call(
        late_kernel,
        out_shape=(up_shape, head_shape),
        in_specs=[smem] + [vmem] * 2 + [hbm] * 8,
        out_specs=(vmem, vmem),
        scratch_shapes=scratch,
        input_output_aliases={1: 0, 2: 1},
    )(early, in_vmem(up), in_vmem(head), *weights)
    (send,) = pl.pallas_call(
        regroup_kernel,
        out_shape=(pltpu.VMEM((NX * NR, 8, 128), BF16),),
        in_specs=[vmem],
        out_specs=(vmem,),
    )(in_vmem(got))
    got = lax.all_to_all(send, ("x", "rep"), 0, 0, tiled=True)
    return pl.pallas_call(
        mask_kernel,
        out_shape=jax.ShapeDtypeStruct((4 * ROWS_T, 4 * EW), F32),
        in_specs=[vmem] * 3,
        out_specs=vmem,
    )(in_vmem(got), in_vmem(up), in_vmem(head))


def solution(mesh):
    split = Mesh(mesh.devices.reshape(NX, NZ, NC, NR), ("x", "z", "core", "rep"))
    tile, every = ("x", "z", "core"), ("x", "z", "core", "rep")
    return jax.shard_map(
        on_device,
        mesh=split,
        in_specs=(
            P(tile, None, None),
            P(every, None),
            P(every),
            P(every),
            P(every, None),
            P(every),
            P(),
            P(),
            P(),
            P(),
            P(),
            P(),
            P(),
        ),
        out_specs=P(tile, None),
        check_vma=False,
    )
```

```python
import math

import jax
import jax.numpy as jnp
from jax import lax
from jax.experimental import pallas as pl
from jax.experimental.pallas import tpu as pltpu
from jax.sharding import Mesh
from jax.sharding import PartitionSpec as P

CK = 4
C = 256
C1 = 64
C2 = 32
ROWS_T = 16
EW = 64
P_DEV = 128
NX, NZ, NC, NR = 4, 16, 2, 4
CELLS = ROWS_T * EW
Z_FIRST, C_FIRST, X_FIRST, R_FIRST = 8, 1, 2, 2
EVERY = ("x", "z", "core", "rep")
F32 = jnp.float32
BF16 = jnp.bfloat16
I32 = jnp.int32


def iota(shape, dim):
    return lax.broadcasted_iota(I32, shape, dim)


def flat(x, z, c, r):
    return ((x % NX * NZ + z % NZ) * NC + c % NC) * NR + r % NR


def exchanged(value, groups):
    return lax.all_to_all(value, EVERY, 0, 0, axis_index_groups=groups, tiled=True)


def column_groups():
    return [
        [flat(x, Z_FIRST + i, C_FIRST + j, r) for i in range(NZ) for j in range(NC)]
        for x in range(NX)
        for r in range(NR)
    ]


def plane_groups():
    return [
        [flat(X_FIRST + i, z, c, R_FIRST + j) for i in range(NX) for j in range(NR)]
        for z in range(NZ)
        for c in range(NC)
    ]


def nt(a, b):
    return lax.dot_general(a, b, (((1,), (1,)), ((), ())), preferred_element_type=F32)


def nn(a, b):
    return jnp.dot(a, b, preferred_element_type=F32)


def gelu(v):
    return 0.5 * v * (1.0 + lax.erf(v * (1.0 / math.sqrt(2.0))))


def local_tables(emb, one, two, pe, bias, w1, w2, w3, up_ref, head_ref):
    q = iota((256, P_DEV), 0)
    first = ((q >> 4).astype(F32) + 0.5) / (4.0 * CK) * 2.0 - 1.0
    second = ((q & 15).astype(F32) + 0.5) / (4.0 * CK) * 2.0 - 1.0
    pe_value = pe[...]
    angles = (first * pe_value[0:1, :] + second * pe_value[1:2, :]) * (2.0 * math.pi)
    tokens = (jnp.concatenate([jnp.sin(angles), jnp.cos(angles)], axis=1) + bias[...]).astype(BF16)
    hidden = jnp.maximum(nn(tokens, w1[...]), 0.0).astype(BF16)
    hidden = jnp.maximum(nn(hidden, w2[...]), 0.0).astype(BF16)
    head_ref[...] = nt(w3[...], hidden).astype(BF16)

    row = iota((512, P_DEV), 0)
    k, x, y = row >> 4, (row >> 2) & 3, row & 3
    pick = (iota((512, P_DEV), 1) == (2 * (y & 1) + (x & 1)) * C2 + k).astype(BF16)
    row = iota((512, 256), 0)
    off = 2 * ((row & 3) >> 1) + (((row >> 2) & 3) >> 1)
    keep = (iota((512, 256), 1) >> 6) == off
    two_tiled = jnp.concatenate([two[...]] * 4, axis=0)
    wide = jnp.where(keep, nt(pick, two_tiled), 0.0).astype(BF16)
    one_t = one[...].astype(F32).T.astype(BF16)

    def block(i, carry):
        start = pl.multiple_of(i * 128, 128)
        first_up = nt(one_t, emb[pl.ds(start, 128), :])
        parts = []
        for o in range(4):
            v = first_up[o * C1 : (o + 1) * C1, :]
            v = v - jnp.mean(v, axis=0, keepdims=True)
            v = v * lax.rsqrt(jnp.mean(v * v, axis=0, keepdims=True) + 1e-06)
            parts.append(gelu(v).astype(BF16))
        active = jnp.concatenate(parts, axis=0)
        up_ref[:, pl.ds(start, 128)] = gelu(nn(wide, active)).astype(BF16)
        return carry

    lax.fori_loop(0, CELLS // 128, block, 0)


def gathered_in(refs, bufs, sems):
    copies = [pltpu.make_async_copy(r, b, sems.at[i]) for i, (r, b) in enumerate(zip(refs, bufs))]
    for c in copies:
        c.start()
    for c in copies:
        c.wait()


def in_vmem(value):
    return pltpu.with_memory_space_constraint(value, pltpu.VMEM)


def is_early():
    return lax.axis_index("z") <= 2


def slots_kernel(early, tile, row, col, pts, conf, *rest):
    weights, (send, up, head), scratch = rest[:8], rest[8:11], rest[11:]
    bufs, sems = scratch[:8], scratch[8]
    t = tile[...]
    names = (iota((P_DEV, P_DEV), 0) == t).astype(F32)
    before = (iota((P_DEV, P_DEV), 0) < iota((P_DEV, P_DEV), 1)).astype(BF16)
    count = nn(names.astype(BF16), before)
    rank = jnp.sum(names * count, axis=0, keepdims=True).astype(I32)
    values = [row[...], col[...], conf[...], pts[0:1, :], pts[1:2, :]]
    group = iota((16, P_DEV), 0)
    x_of, s_of = group >> 2, group & 3
    dest = iota((NZ * NC, P_DEV), 0)

    def part(target, rank_at, values):
        mask = ((target >> 5) == x_of) & (rank_at == s_of)
        rows = [jnp.where(mask, v.astype(F32), 0.0) for v in values]
        rows += [jnp.zeros((16, P_DEV), F32)] * 3
        z, c = (target >> 1) - Z_FIRST, target - C_FIRST
        place = 2 * (z & 15) + (c & 1)
        return nt((place == dest).astype(BF16), jnp.concatenate(rows, axis=0).astype(BF16))

    out = part(t, rank, values) + part(t + 1, rank + 2, [values[0] - ROWS_T] + values[1:])
    send[...] = out.reshape(NZ * NC, 1, 128)

    @pl.when(early[0] == 1)
    def _():
        gathered_in(weights, bufs, sems)
        local_tables(*bufs, up, head)


def late_kernel(early, up_in, head_in, *rest):
    weights, (up, head), scratch = rest[:8], rest[8:10], rest[10:]
    bufs, sems = scratch[:8], scratch[8]

    @pl.when(early[0] != 1)
    def _():
        gathered_in(weights, bufs, sems)
        local_tables(*bufs, up, head)


def regroup_kernel(got, send):
    r = got[...].reshape(NZ * NC, 128)
    r = jnp.concatenate([r] * 4, axis=0)
    keep = (iota((128, 128), 1) & 3) == (iota((128, 128), 0) >> 5)
    r = jnp.where(keep, r, 0.0).astype(BF16)
    at, lane = iota((32, 128), 0), iota((32, 128), 1)
    pick = ((lane >> 4) == (at & 7)) & (((lane >> 2) & 3) == (at >> 3))
    out = nt(pick.astype(BF16), r)
    for i in range(NX):
        x = (X_FIRST + i) % NX
        for j in range(NR):
            send[i * NR + j] = out[x * 8 : (x + 1) * 8, :].astype(BF16)


def mask_kernel(got, up, head, out):
    lane = iota((8, 128), 1)
    own, below = [], []
    for j in range(8):
        a, b = got[j].astype(F32), got[j + 8].astype(F32)
        own.append(jnp.where(lane < 64, a, pltpu.roll(b, 64, 1)))
        below.append(jnp.where(lane < 64, pltpu.roll(a, 64, 1), b))
    own, below = jnp.concatenate(own, axis=1), jnp.concatenate(below, axis=1)
    many = 1024
    r_at = iota((16, many), 0).astype(F32)
    c_at = iota((EW, many), 0).astype(F32)
    table = head[...]

    def one_hot(v, at):
        return (at == v).astype(BF16)

    def factors(v, rows):
        row, col, conf, first, second = (v[i : i + 1, :] for i in range(5))
        hot_a, hot_b = one_hot(first, r_at), one_hot(second, r_at)
        hot = jnp.concatenate([hot_a[i : i + 1, :] * hot_b for i in range(16)], axis=0)
        heads = nn(table, hot).astype(BF16)
        d = r_at - row
        in_row = ((d >= 0.0) & (d <= 3.0)).astype(BF16)
        d = c_at - col
        in_col = jnp.where((d >= 0.0) & (d <= 3.0), conf, 0.0).astype(BF16)
        blank = jnp.zeros((EW, many), BF16)
        even, odd = jnp.concatenate([in_col, blank], axis=0), jnp.concatenate([blank, in_col], axis=0)
        lefts = [heads * in_row[i : i + 1, :] for i in range(rows)]
        return (
            nt(jnp.concatenate(lefts[0::2], axis=0), even)
            + nt(jnp.concatenate(lefts[1::2], axis=0), odd)
        )

    total = factors(own, 16)
    spill = factors(below, 4)
    total = jnp.concatenate([total[:64] + spill, total[64:]], axis=0)

    sub = iota((8, 128), 0)
    mine = (sub >> 2) == (iota((8, 128), 1) >> 6)
    blocks = []
    for j in range(8):
        h = total[j * 32 : (j + 1) * 32, :]
        low, high = jnp.zeros((8, 128), F32), jnp.zeros((8, 128), F32)
        for k in range(C2):
            u = up[k * 16 : (k + 1) * 16, j * 128 : (j + 1) * 128].astype(F32)
            w = h[k : k + 1, :]
            low, high = low + u[:8] * w, high + u[8:] * w
        pieces = []
        for v in (low, high):
            turned = pltpu.roll(v, 4, 0)
            pieces.append(jnp.where(mine, jnp.where(sub < 4, v, turned), 0.0))
            pieces.append(jnp.where(mine, jnp.where(sub < 4, turned, v), 0.0))
        blocks.append(jnp.concatenate(pieces, axis=1))
    flat = jnp.concatenate(blocks, axis=0) * 0.25
    at, lane = iota((512, 256), 0), iota((512, 256), 1)
    spread = (lane == 4 * (at & 63) + (at >> 7)).astype(BF16)
    top = flat.astype(BF16)
    rest = flat - top.astype(F32)
    mid = rest.astype(BF16)
    last = (rest - mid.astype(F32)).astype(BF16)
    out[...] = nn(top, spread) + (nn(mid, spread) + nn(last, spread))


def on_device(
    embedding,
    prompt_tile,
    crop_row,
    crop_col,
    points,
    confidence,
    pe_matrix,
    point_embed,
    w_one,
    w_two,
    w_three,
    conv_one,
    conv_two,
):
    early = is_early().astype(I32).reshape(1)
    smem = pl.BlockSpec(memory_space=pltpu.SMEM)
    vmem = pl.BlockSpec(memory_space=pltpu.VMEM)
    hbm = pl.BlockSpec(memory_space=pl.ANY)
    weights = (
        embedding.reshape(CELLS, C),
        conv_one,
        conv_two,
        pe_matrix,
        point_embed.reshape(1, 256),
        w_one,
        w_two,
        w_three.T,
    )
    up_shape = pltpu.VMEM((16 * C2, CELLS), BF16)
    head_shape = pltpu.VMEM((C2, 256), BF16)
    scratch = [pltpu.VMEM(w.shape, w.dtype) for w in weights] + [pltpu.SemaphoreType.DMA((8,))]
    send, up, head = pl.pallas_call(
        slots_kernel,
        out_shape=(pltpu.VMEM((NZ * NC, 1, 128), F32), up_shape, head_shape),
        in_specs=[smem] + [vmem] * 5 + [hbm] * 8,
        out_specs=(vmem, vmem, vmem),
        scratch_shapes=scratch,
    )(
        early,
        prompt_tile.reshape(1, P_DEV),
        crop_row.reshape(1, P_DEV),
        crop_col.reshape(1, P_DEV),
        points.T,
        confidence.reshape(1, P_DEV),
        *weights,
    )
    got = exchanged(send, column_groups())
    up, head = pl.pallas_call(
        late_kernel,
        out_shape=(up_shape, head_shape),
        in_specs=[smem] + [vmem] * 2 + [hbm] * 8,
        out_specs=(vmem, vmem),
        scratch_shapes=scratch,
        input_output_aliases={1: 0, 2: 1},
    )(early, in_vmem(up), in_vmem(head), *weights)
    (send,) = pl.pallas_call(
        regroup_kernel,
        out_shape=(pltpu.VMEM((NX * NR, 8, 128), BF16),),
        in_specs=[vmem],
        out_specs=(vmem,),
    )(in_vmem(got))
    got = exchanged(send, plane_groups())
    return pl.pallas_call(
        mask_kernel,
        out_shape=jax.ShapeDtypeStruct((4 * ROWS_T, 4 * EW), F32),
        in_specs=[vmem] * 3,
        out_specs=vmem,
    )(in_vmem(got), in_vmem(up), in_vmem(head))


def solution(mesh):
    split = Mesh(mesh.devices.reshape(NX, NZ, NC, NR), EVERY)
    tile, every = EVERY[:3], EVERY
    return jax.shard_map(
        on_device,
        mesh=split,
        in_specs=(
            P(tile, None, None),
            P(every, None),
            P(every),
            P(every),
            P(every, None),
            P(every),
            P(),
            P(),
            P(),
            P(),
            P(),
            P(),
            P(),
        ),
        out_specs=P(tile, None),
        check_vma=False,
    )
```

```python
import math

import jax
import jax.numpy as jnp
from jax import lax
from jax.experimental import pallas as pl
from jax.experimental.pallas import tpu as pltpu
from jax.sharding import Mesh
from jax.sharding import PartitionSpec as P

CK = 4
C = 256
C1 = 64
C2 = 32
ROWS_T = 16
EW = 64
P_DEV = 128
NX, NZ, NC, NR = 4, 16, 2, 4
CELLS = ROWS_T * EW
Z_FIRST, C_FIRST, X_FIRST, R_FIRST = 8, 1, 2, 2
EVERY = ("x", "z", "core", "rep")
F32 = jnp.float32
BF16 = jnp.bfloat16
I32 = jnp.int32


def iota(shape, dim):
    return lax.broadcasted_iota(I32, shape, dim)


def flat(x, z, c, r):
    return ((x % NX * NZ + z % NZ) * NC + c % NC) * NR + r % NR


def exchanged(value, groups):
    return lax.all_to_all(value, EVERY, 0, 0, axis_index_groups=groups, tiled=True)


def column_groups():
    return [
        [flat(x, Z_FIRST + i, C_FIRST + j, r) for i in range(NZ) for j in range(NC)]
        for x in range(NX)
        for r in range(NR)
    ]


def plane_groups():
    return [
        [flat(X_FIRST + i, z, c, R_FIRST + j) for i in range(NX) for j in range(NR)]
        for z in range(NZ)
        for c in range(NC)
    ]


def nt(a, b):
    return lax.dot_general(a, b, (((1,), (1,)), ((), ())), preferred_element_type=F32)


def nn(a, b):
    return jnp.dot(a, b, preferred_element_type=F32)


def gelu(v):
    return 0.5 * v * (1.0 + lax.erf(v * (1.0 / math.sqrt(2.0))))


def local_tables(emb, one, two, pe, bias, w1, w2, w3, up_ref, head_ref):
    q = iota((256, P_DEV), 0)
    first = ((q >> 4).astype(F32) + 0.5) / (4.0 * CK) * 2.0 - 1.0
    second = ((q & 15).astype(F32) + 0.5) / (4.0 * CK) * 2.0 - 1.0
    pe_value = pe[...]
    angles = (first * pe_value[0:1, :] + second * pe_value[1:2, :]) * (2.0 * math.pi)
    tokens = (jnp.concatenate([jnp.sin(angles), jnp.cos(angles)], axis=1) + bias[...]).astype(BF16)
    hidden = jnp.maximum(nn(tokens, w1[...]), 0.0).astype(BF16)
    hidden = jnp.maximum(nn(hidden, w2[...]), 0.0).astype(BF16)
    head_ref[...] = nt(w3[...], hidden).astype(BF16)

    row = iota((512, P_DEV), 0)
    k, x, y = row >> 4, (row >> 2) & 3, row & 3
    pick = (iota((512, P_DEV), 1) == (2 * (y & 1) + (x & 1)) * C2 + k).astype(BF16)
    row = iota((512, 256), 0)
    off = 2 * ((row & 3) >> 1) + (((row >> 2) & 3) >> 1)
    keep = (iota((512, 256), 1) >> 6) == off
    two_tiled = jnp.concatenate([two[...]] * 4, axis=0)
    wide = jnp.where(keep, nt(pick, two_tiled), 0.0).astype(BF16)
    one_t = one[...].astype(F32).T.astype(BF16)

    def block(i, carry):
        start = pl.multiple_of(i * 128, 128)
        first_up = nt(one_t, emb[pl.ds(start, 128), :])
        parts = []
        for o in range(4):
            v = first_up[o * C1 : (o + 1) * C1, :]
            v = v - jnp.mean(v, axis=0, keepdims=True)
            v = v * lax.rsqrt(jnp.mean(v * v, axis=0, keepdims=True) + 1e-06)
            parts.append(gelu(v).astype(BF16))
        active = jnp.concatenate(parts, axis=0)
        up_ref[:, pl.ds(start, 128)] = gelu(nn(wide, active)).astype(BF16)
        return carry

    lax.fori_loop(0, CELLS // 128, block, 0)


def gathered_in(refs, bufs, sems):
    copies = [pltpu.make_async_copy(r, b, sems.at[i]) for i, (r, b) in enumerate(zip(refs, bufs))]
    for c in copies:
        c.start()
    for c in copies:
        c.wait()


def in_vmem(value):
    return pltpu.with_memory_space_constraint(value, pltpu.VMEM)


def is_early():
    at = [lax.axis_index(a) for a in EVERY]
    return (at[1] <= 3) & (at[0] + at[1] + at[2] + at[3] > 0)


def slots_kernel(early, tile, row, col, pts, conf, *rest):
    weights, (send, up, head), scratch = rest[:8], rest[8:11], rest[11:]
    bufs, sems = scratch[:8], scratch[8]
    t = tile[...]
    names = (iota((P_DEV, P_DEV), 0) == t).astype(F32)
    before = (iota((P_DEV, P_DEV), 0) < iota((P_DEV, P_DEV), 1)).astype(BF16)
    count = nn(names.astype(BF16), before)
    rank = jnp.sum(names * count, axis=0, keepdims=True).astype(I32)
    values = [row[...], col[...], conf[...], pts[0:1, :], pts[1:2, :]]
    group = iota((16, P_DEV), 0)
    x_of, s_of = group >> 2, group & 3
    dest = iota((NZ * NC, P_DEV), 0)

    def part(target, rank_at, values):
        mask = ((target >> 5) == x_of) & (rank_at == s_of)
        rows = [jnp.where(mask, v.astype(F32), 0.0) for v in values]
        rows += [jnp.zeros((16, P_DEV), F32)] * 3
        z, c = (target >> 1) - Z_FIRST, target - C_FIRST
        place = 2 * (z & 15) + (c & 1)
        return nt((place == dest).astype(BF16), jnp.concatenate(rows, axis=0).astype(BF16))

    out = part(t, rank, values) + part(t + 1, rank + 2, [values[0] - ROWS_T] + values[1:])
    send[...] = out.reshape(NZ * NC, 1, 128)

    @pl.when(early[0] == 1)
    def _():
        gathered_in(weights, bufs, sems)
        local_tables(*bufs, up, head)


def late_kernel(early, up_in, head_in, *rest):
    weights, (up, head), scratch = rest[:8], rest[8:10], rest[10:]
    bufs, sems = scratch[:8], scratch[8]

    @pl.when(early[0] != 1)
    def _():
        gathered_in(weights, bufs, sems)
        local_tables(*bufs, up, head)


def regroup_kernel(got, send):
    r = got[...].reshape(NZ * NC, 128)
    r = jnp.concatenate([r] * 4, axis=0)
    keep = (iota((128, 128), 1) & 3) == (iota((128, 128), 0) >> 5)
    r = jnp.where(keep, r, 0.0).astype(BF16)
    at, lane = iota((32, 128), 0), iota((32, 128), 1)
    pick = ((lane >> 4) == (at & 7)) & (((lane >> 2) & 3) == (at >> 3))
    out = nt(pick.astype(BF16), r)
    for i in range(NX):
        x = (X_FIRST + i) % NX
        for j in range(NR):
            send[i * NR + j] = out[x * 8 : (x + 1) * 8, :].astype(BF16)


def mask_kernel(got, up, head, out):
    lane = iota((8, 128), 1)
    own, below = [], []
    for j in range(8):
        a, b = got[j].astype(F32), got[j + 8].astype(F32)
        own.append(jnp.where(lane < 64, a, pltpu.roll(b, 64, 1)))
        below.append(jnp.where(lane < 64, pltpu.roll(a, 64, 1), b))
    own, below = jnp.concatenate(own, axis=1), jnp.concatenate(below, axis=1)
    many = 1024
    r_at = iota((16, many), 0).astype(F32)
    c_at = iota((EW, many), 0).astype(F32)
    table = head[...]

    def one_hot(v, at):
        return (at == v).astype(BF16)

    def factors(v, rows):
        row, col, conf, first, second = (v[i : i + 1, :] for i in range(5))
        hot_a, hot_b = one_hot(first, r_at), one_hot(second, r_at)
        hot = jnp.concatenate([hot_a[i : i + 1, :] * hot_b for i in range(16)], axis=0)
        heads = nn(table, hot).astype(BF16)
        d = r_at - row
        in_row = ((d >= 0.0) & (d <= 3.0)).astype(BF16)
        d = c_at - col
        in_col = jnp.where((d >= 0.0) & (d <= 3.0), conf, 0.0).astype(BF16)
        blank = jnp.zeros((EW, many), BF16)
        even, odd = jnp.concatenate([in_col, blank], axis=0), jnp.concatenate([blank, in_col], axis=0)
        lefts = [heads * in_row[i : i + 1, :] for i in range(rows)]
        return (
            nt(jnp.concatenate(lefts[0::2], axis=0), even)
            + nt(jnp.concatenate(lefts[1::2], axis=0), odd)
        )

    total = factors(own, 16)
    spill = factors(below, 4)
    total = jnp.concatenate([total[:64] + spill, total[64:]], axis=0)

    sub = iota((8, 128), 0)
    mine = (sub >> 2) == (iota((8, 128), 1) >> 6)
    blocks = []
    for j in range(8):
        h = total[j * 32 : (j + 1) * 32, :]
        low, high = jnp.zeros((8, 128), F32), jnp.zeros((8, 128), F32)
        for k in range(C2):
            u = up[k * 16 : (k + 1) * 16, j * 128 : (j + 1) * 128].astype(F32)
            w = h[k : k + 1, :]
            low, high = low + u[:8] * w, high + u[8:] * w
        pieces = []
        for v in (low, high):
            turned = pltpu.roll(v, 4, 0)
            pieces.append(jnp.where(mine, jnp.where(sub < 4, v, turned), 0.0))
            pieces.append(jnp.where(mine, jnp.where(sub < 4, turned, v), 0.0))
        blocks.append(jnp.concatenate(pieces, axis=1))
    flat = jnp.concatenate(blocks, axis=0) * 0.25
    at, lane = iota((512, 256), 0), iota((512, 256), 1)
    spread = (lane == 4 * (at & 63) + (at >> 7)).astype(BF16)
    top = flat.astype(BF16)
    rest = flat - top.astype(F32)
    mid = rest.astype(BF16)
    last = (rest - mid.astype(F32)).astype(BF16)
    out[...] = nn(top, spread) + (nn(mid, spread) + nn(last, spread))


def on_device(
    embedding,
    prompt_tile,
    crop_row,
    crop_col,
    points,
    confidence,
    pe_matrix,
    point_embed,
    w_one,
    w_two,
    w_three,
    conv_one,
    conv_two,
):
    early = is_early().astype(I32).reshape(1)
    smem = pl.BlockSpec(memory_space=pltpu.SMEM)
    vmem = pl.BlockSpec(memory_space=pltpu.VMEM)
    hbm = pl.BlockSpec(memory_space=pl.ANY)
    weights = (
        embedding.reshape(CELLS, C),
        conv_one,
        conv_two,
        pe_matrix,
        point_embed.reshape(1, 256),
        w_one,
        w_two,
        w_three.T,
    )
    up_shape = pltpu.VMEM((16 * C2, CELLS), BF16)
    head_shape = pltpu.VMEM((C2, 256), BF16)
    scratch = [pltpu.VMEM(w.shape, w.dtype) for w in weights] + [pltpu.SemaphoreType.DMA((8,))]
    send, up, head = pl.pallas_call(
        slots_kernel,
        out_shape=(pltpu.VMEM((NZ * NC, 1, 128), F32), up_shape, head_shape),
        in_specs=[smem] + [vmem] * 5 + [hbm] * 8,
        out_specs=(vmem, vmem, vmem),
        scratch_shapes=scratch,
    )(
        early,
        prompt_tile.reshape(1, P_DEV),
        crop_row.reshape(1, P_DEV),
        crop_col.reshape(1, P_DEV),
        points.T,
        confidence.reshape(1, P_DEV),
        *weights,
    )
    got = exchanged(send, column_groups())
    up, head = pl.pallas_call(
        late_kernel,
        out_shape=(up_shape, head_shape),
        in_specs=[smem] + [vmem] * 2 + [hbm] * 8,
        out_specs=(vmem, vmem),
        scratch_shapes=scratch,
        input_output_aliases={1: 0, 2: 1},
    )(early, in_vmem(up), in_vmem(head), *weights)
    (send,) = pl.pallas_call(
        regroup_kernel,
        out_shape=(pltpu.VMEM((NX * NR, 8, 128), BF16),),
        in_specs=[vmem],
        out_specs=(vmem,),
    )(in_vmem(got))
    got = exchanged(send, plane_groups())
    return pl.pallas_call(
        mask_kernel,
        out_shape=jax.ShapeDtypeStruct((4 * ROWS_T, 4 * EW), F32),
        in_specs=[vmem] * 3,
        out_specs=vmem,
    )(in_vmem(got), in_vmem(up), in_vmem(head))


def solution(mesh):
    split = Mesh(mesh.devices.reshape(NX, NZ, NC, NR), EVERY)
    tile, every = EVERY[:3], EVERY
    return jax.shard_map(
        on_device,
        mesh=split,
        in_specs=(
            P(tile, None, None),
            P(every, None),
            P(every),
            P(every),
            P(every, None),
            P(every),
            P(),
            P(),
            P(),
            P(),
            P(),
            P(),
            P(),
        ),
        out_specs=P(tile, None),
        check_vma=False,
    )
```

```python
import math

import jax
import jax.numpy as jnp
from jax import lax
from jax.experimental import pallas as pl
from jax.experimental.pallas import tpu as pltpu
from jax.sharding import Mesh
from jax.sharding import PartitionSpec as P

CK = 4
C = 256
C1 = 64
C2 = 32
ROWS_T = 16
EW = 64
P_DEV = 128
NX, NZ, NC, NR = 4, 16, 2, 4
CELLS = ROWS_T * EW
Z_FIRST, C_FIRST, X_FIRST, R_FIRST = 8, 1, 2, 2
UNROLL, BLOCK = 4, 256
EVERY = ("x", "z", "core", "rep")
F32 = jnp.float32
BF16 = jnp.bfloat16
I32 = jnp.int32


def iota(shape, dim):
    return lax.broadcasted_iota(I32, shape, dim)


def flat(x, z, c, r):
    return ((x % NX * NZ + z % NZ) * NC + c % NC) * NR + r % NR


def exchanged(value, groups):
    return lax.all_to_all(value, EVERY, 0, 0, axis_index_groups=groups, tiled=True)


def column_groups():
    return [
        [flat(x, Z_FIRST + i, C_FIRST + j, r) for i in range(NZ) for j in range(NC)]
        for x in range(NX)
        for r in range(NR)
    ]


def plane_groups():
    return [
        [flat(X_FIRST + i, z, c, R_FIRST + j) for i in range(NX) for j in range(NR)]
        for z in range(NZ)
        for c in range(NC)
    ]


def nt(a, b):
    return lax.dot_general(a, b, (((1,), (1,)), ((), ())), preferred_element_type=F32)


def nn(a, b):
    return jnp.dot(a, b, preferred_element_type=F32)


def gelu(v):
    return 0.5 * v * (1.0 + lax.erf(v * (1.0 / math.sqrt(2.0))))


def local_tables(emb, one, two, pe, bias, w1, w2, w3, up_ref, head_ref):
    coord = (iota((16, P_DEV), 0).astype(F32) + 0.5) / (4.0 * CK) * 2.0 - 1.0
    angle_a = coord * pe[0:1, :] * (2.0 * math.pi)
    angle_b = coord * pe[1:2, :] * (2.0 * math.pi)
    sin_a, cos_a, sin_b, cos_b = jnp.sin(angle_a), jnp.cos(angle_a), jnp.sin(angle_b), jnp.cos(angle_b)
    sines, cosines = [], []
    for i in range(16):
        sin_i, cos_i = sin_a[i : i + 1, :], cos_a[i : i + 1, :]
        sines.append(sin_i * cos_b + cos_i * sin_b)
        cosines.append(cos_i * cos_b - sin_i * sin_b)
    sines, cosines = jnp.concatenate(sines, axis=0), jnp.concatenate(cosines, axis=0)
    tokens = (jnp.concatenate([sines, cosines], axis=1) + bias[...]).astype(BF16)
    hidden = jnp.maximum(nn(tokens, w1[...]), 0.0).astype(BF16)
    hidden = jnp.maximum(nn(hidden, w2[...]), 0.0).astype(BF16)
    head_ref[...] = nt(w3[...], hidden).astype(BF16)

    row = iota((16, P_DEV), 0)
    x, y = row >> 2, row & 3
    ahead = iota((16, P_DEV), 1) - (2 * (y & 1) + (x & 1)) * C2
    pick = jnp.concatenate([(ahead == k).astype(F32) for k in range(C2)], axis=0).astype(BF16)
    row = iota((16, 256), 0)
    keep = (iota((16, 256), 1) >> 6) == 2 * ((row & 3) >> 1) + (row >> 3)
    spread = nt(pick, jnp.concatenate([two[...]] * 4, axis=0))
    wide = [jnp.where(keep, spread[16 * k : 16 * k + 16], 0.0) for k in range(C2)]
    wide = jnp.concatenate(wide, axis=0).astype(BF16)
    one_t = one[...].astype(F32).T.astype(BF16)

    def block(i, carry):
        start = pl.multiple_of(i * BLOCK, BLOCK)
        first_up = nt(one_t, emb[pl.ds(start, BLOCK), :])
        parts = []
        for o in range(4):
            v = first_up[o * C1 : (o + 1) * C1, :]
            v = v - jnp.mean(v, axis=0, keepdims=True)
            v = v * lax.rsqrt(jnp.mean(v * v, axis=0, keepdims=True) + 1e-06)
            parts.append(gelu(v).astype(BF16))
        active = jnp.concatenate(parts, axis=0)
        up_ref[:, pl.ds(start, BLOCK)] = gelu(nn(wide, active)).astype(BF16)
        return carry

    lax.fori_loop(0, CELLS // BLOCK, block, 0, unroll=UNROLL)


def gathered_in(refs, bufs, sems):
    copies = [pltpu.make_async_copy(r, b, sems.at[i]) for i, (r, b) in enumerate(zip(refs, bufs))]
    for c in copies:
        c.start()
    for c in copies:
        c.wait()


def in_vmem(value):
    return pltpu.with_memory_space_constraint(value, pltpu.VMEM)


def is_early():
    at = [lax.axis_index(a) for a in EVERY]
    return (at[1] <= 7) & (at[0] + at[1] + at[2] + at[3] > 0)


def slots_kernel(early, tile, row, col, pts, conf, *rest):
    weights, (send, up, head), scratch = rest[:8], rest[8:11], rest[11:]
    bufs, sems = scratch[:8], scratch[8]
    t = tile[...]
    names = (iota((P_DEV, P_DEV), 0) == t).astype(F32)
    before = (iota((P_DEV, P_DEV), 0) < iota((P_DEV, P_DEV), 1)).astype(BF16)
    count = nn(names.astype(BF16), before)
    rank = jnp.sum(names * count, axis=0, keepdims=True).astype(I32)
    values = [row[...], col[...], conf[...], pts[0:1, :], pts[1:2, :]]
    group = iota((16, P_DEV), 0)
    x_of, s_of = group >> 2, group & 3
    dest = iota((NZ * NC, P_DEV), 0)

    def part(target, rank_at, values):
        mask = ((target >> 5) == x_of) & (rank_at == s_of)
        rows = [jnp.where(mask, v.astype(F32), 0.0) for v in values]
        rows += [jnp.zeros((16, P_DEV), F32)] * 3
        z, c = (target >> 1) - Z_FIRST, target - C_FIRST
        place = 2 * (z & 15) + (c & 1)
        return nt((place == dest).astype(BF16), jnp.concatenate(rows, axis=0).astype(BF16))

    out = part(t, rank, values) + part(t + 1, rank + 2, [values[0] - ROWS_T] + values[1:])
    send[...] = out.reshape(NZ * NC, 1, 128)

    @pl.when(early[0] == 1)
    def _():
        gathered_in(weights, bufs, sems)
        local_tables(*bufs, up, head)


def late_kernel(early, up_in, head_in, *rest):
    weights, (up, head), scratch = rest[:8], rest[8:10], rest[10:]
    bufs, sems = scratch[:8], scratch[8]

    @pl.when(early[0] != 1)
    def _():
        gathered_in(weights, bufs, sems)
        local_tables(*bufs, up, head)


def regroup_kernel(got, send, spare):
    spare[...] = jnp.zeros((8, 128), F32)
    r = got[...].reshape(NZ * NC, 128)
    r = jnp.concatenate([r] * 4, axis=0)
    keep = (iota((128, 128), 1) & 3) == (iota((128, 128), 0) >> 5)
    r = jnp.where(keep, r, 0.0).astype(BF16)
    at, lane = iota((32, 128), 0), iota((32, 128), 1)
    pick = ((lane >> 4) == (at & 7)) & (((lane >> 2) & 3) == (at >> 3))
    out = nt(pick.astype(BF16), r)
    for i in range(NX):
        x = (X_FIRST + i) % NX
        for j in range(NR):
            send[i * NR + j] = out[x * 8 : (x + 1) * 8, :].astype(BF16)


def mask_kernel(got, up, head, out):
    lane = iota((8, 128), 1)
    own, below = [], []
    for j in range(8):
        a, b = got[j].astype(F32), got[j + 8].astype(F32)
        own.append(jnp.where(lane < 64, a, pltpu.roll(b, 64, 1)))
        below.append(jnp.where(lane < 64, pltpu.roll(a, 64, 1), b))
    own, below = jnp.concatenate(own, axis=1), jnp.concatenate(below, axis=1)
    many = 1024
    r_at = iota((16, many), 0).astype(F32)
    c_at = iota((EW, many), 0).astype(F32)
    table = head[...]

    def one_hot(v, at):
        return (at == v).astype(BF16)

    def factors(v, rows):
        row, col, conf, first, second = (v[i : i + 1, :] for i in range(5))
        hot_a, hot_b = one_hot(first, r_at), one_hot(second, r_at)
        hot = jnp.concatenate([hot_a[i : i + 1, :] * hot_b for i in range(16)], axis=0)
        heads = nn(table, hot).astype(BF16)
        d = r_at - row
        in_row = ((d >= 0.0) & (d <= 3.0)).astype(BF16)
        d = c_at - col
        in_col = jnp.where((d >= 0.0) & (d <= 3.0), conf, 0.0).astype(BF16)
        blank = jnp.zeros((EW, many), BF16)
        even, odd = jnp.concatenate([in_col, blank], axis=0), jnp.concatenate([blank, in_col], axis=0)
        lefts = [heads * in_row[i : i + 1, :] for i in range(rows)]
        return (
            nt(jnp.concatenate(lefts[0::2], axis=0), even)
            + nt(jnp.concatenate(lefts[1::2], axis=0), odd)
        )

    total = factors(own, 16)
    spill = factors(below, 4)
    total = jnp.concatenate([total[:64] + spill, total[64:]], axis=0)

    sub = iota((8, 128), 0)
    mine = (sub >> 2) == (iota((8, 128), 1) >> 6)
    blocks = []
    for j in range(8):
        h = total[j * 32 : (j + 1) * 32, :]
        low, high = jnp.zeros((8, 128), F32), jnp.zeros((8, 128), F32)
        for k in range(C2):
            u = up[k * 16 : (k + 1) * 16, j * 128 : (j + 1) * 128].astype(F32)
            w = h[k : k + 1, :]
            low, high = low + u[:8] * w, high + u[8:] * w
        pieces = []
        for v in (low, high):
            turned = pltpu.roll(v, 4, 0)
            pieces.append(jnp.where(mine, jnp.where(sub < 4, v, turned), 0.0))
            pieces.append(jnp.where(mine, jnp.where(sub < 4, turned, v), 0.0))
        blocks.append(jnp.concatenate(pieces, axis=1))
    flat = jnp.concatenate(blocks, axis=0) * 0.25
    at, lane = iota((512, 256), 0), iota((512, 256), 1)
    spread = (lane == 4 * (at & 63) + (at >> 7)).astype(BF16)
    top = flat.astype(BF16)
    rest = flat - top.astype(F32)
    mid = rest.astype(BF16)
    last = (rest - mid.astype(F32)).astype(BF16)
    out[...] = nn(top, spread) + (nn(mid, spread) + nn(last, spread))


def on_device(
    embedding,
    prompt_tile,
    crop_row,
    crop_col,
    points,
    confidence,
    pe_matrix,
    point_embed,
    w_one,
    w_two,
    w_three,
    conv_one,
    conv_two,
):
    early = is_early().astype(I32).reshape(1)
    smem = pl.BlockSpec(memory_space=pltpu.SMEM)
    vmem = pl.BlockSpec(memory_space=pltpu.VMEM)
    hbm = pl.BlockSpec(memory_space=pl.ANY)
    weights = (
        embedding.reshape(CELLS, C),
        conv_one,
        conv_two,
        pe_matrix,
        point_embed.reshape(1, 256),
        w_one,
        w_two,
        w_three.T,
    )
    up_shape = pltpu.VMEM((16 * C2, CELLS), BF16)
    head_shape = pltpu.VMEM((C2, 256), BF16)
    scratch = [pltpu.VMEM(w.shape, w.dtype) for w in weights] + [pltpu.SemaphoreType.DMA((8,))]
    send, up, head = pl.pallas_call(
        slots_kernel,
        out_shape=(pltpu.VMEM((NZ * NC, 1, 128), F32), up_shape, head_shape),
        in_specs=[smem] + [vmem] * 5 + [hbm] * 8,
        out_specs=(vmem, vmem, vmem),
        scratch_shapes=scratch,
    )(
        early,
        prompt_tile.reshape(1, P_DEV),
        crop_row.reshape(1, P_DEV),
        crop_col.reshape(1, P_DEV),
        points.T,
        confidence.reshape(1, P_DEV),
        *weights,
    )
    got = exchanged(send, column_groups())
    up, head = pl.pallas_call(
        late_kernel,
        out_shape=(up_shape, head_shape),
        in_specs=[smem] + [vmem] * 2 + [hbm] * 8,
        out_specs=(vmem, vmem),
        scratch_shapes=scratch,
        input_output_aliases={1: 0, 2: 1},
    )(early, in_vmem(up), in_vmem(head), *weights)
    send, _ = pl.pallas_call(
        regroup_kernel,
        out_shape=(pltpu.VMEM((NX * NR, 8, 128), BF16), pltpu.VMEM((8, 128), F32)),
        in_specs=[vmem],
        out_specs=(vmem, vmem),
    )(in_vmem(got))
    got = exchanged(send, plane_groups())
    return pl.pallas_call(
        mask_kernel,
        out_shape=jax.ShapeDtypeStruct((4 * ROWS_T, 4 * EW), F32),
        in_specs=[vmem] * 3,
        out_specs=vmem,
    )(in_vmem(got), in_vmem(up), in_vmem(head))


def solution(mesh):
    split = Mesh(mesh.devices.reshape(NX, NZ, NC, NR), EVERY)
    tile, every = EVERY[:3], EVERY
    return jax.shard_map(
        on_device,
        mesh=split,
        in_specs=(
            P(tile, None, None),
            P(every, None),
            P(every),
            P(every),
            P(every, None),
            P(every),
            P(),
            P(),
            P(),
            P(),
            P(),
            P(),
            P(),
        ),
        out_specs=P(tile, None),
        check_vma=False,
    )
```

```python
import math

import jax
import jax.numpy as jnp
from jax import lax
from jax.experimental import pallas as pl
from jax.experimental.pallas import tpu as pltpu
from jax.sharding import Mesh
from jax.sharding import PartitionSpec as P

CK = 4
C = 256
C1 = 64
C2 = 32
ROWS_T = 16
EW = 64
P_DEV = 128
NX, NZ, NC, NR = 4, 16, 2, 4
CELLS = ROWS_T * EW
Z_FIRST, C_FIRST, X_FIRST, R_FIRST = 8, 1, 2, 2
UNROLL, BLOCK = 4, 256
EVERY = ("x", "z", "core", "rep")
F32 = jnp.float32
BF16 = jnp.bfloat16
I32 = jnp.int32


def iota(shape, dim):
    return lax.broadcasted_iota(I32, shape, dim)


def flat(x, z, c, r):
    return ((x % NX * NZ + z % NZ) * NC + c % NC) * NR + r % NR


def exchanged(value, groups):
    return lax.all_to_all(value, EVERY, 0, 0, axis_index_groups=groups, tiled=True)


def column_groups():
    return [
        [flat(x, Z_FIRST + i, C_FIRST + j, r) for i in range(NZ) for j in range(NC)]
        for x in range(NX)
        for r in range(NR)
    ]


def plane_groups():
    return [
        [flat(X_FIRST + i, z, c, R_FIRST + j) for i in range(NX) for j in range(NR)]
        for z in range(NZ)
        for c in range(NC)
    ]


def nt(a, b):
    return lax.dot_general(a, b, (((1,), (1,)), ((), ())), preferred_element_type=F32)


def nn(a, b):
    return jnp.dot(a, b, preferred_element_type=F32)


def gelu(v):
    return 0.5 * v * (1.0 + lax.erf(v * (1.0 / math.sqrt(2.0))))


def local_tables(emb, one, two, pe, bias, w1, w2, w3, up_ref, head_ref, spread_ref):
    coord = (iota((16, P_DEV), 0).astype(F32) + 0.5) / (4.0 * CK) * 2.0 - 1.0
    angle_a = coord * pe[0:1, :] * (2.0 * math.pi)
    angle_b = coord * pe[1:2, :] * (2.0 * math.pi)
    sin_a, cos_a, sin_b, cos_b = jnp.sin(angle_a), jnp.cos(angle_a), jnp.sin(angle_b), jnp.cos(angle_b)
    sines, cosines = [], []
    for i in range(16):
        sin_i, cos_i = sin_a[i : i + 1, :], cos_a[i : i + 1, :]
        sines.append(sin_i * cos_b + cos_i * sin_b)
        cosines.append(cos_i * cos_b - sin_i * sin_b)
    sines, cosines = jnp.concatenate(sines, axis=0), jnp.concatenate(cosines, axis=0)
    tokens = (jnp.concatenate([sines, cosines], axis=1) + bias[...]).astype(BF16)
    hidden = jnp.maximum(nn(tokens, w1[...]), 0.0).astype(BF16)
    hidden = jnp.maximum(nn(hidden, w2[...]), 0.0).astype(BF16)
    head_ref[...] = nt(w3[...], hidden).astype(BF16)

    same = (iota((128, 128), 0) == iota((128, 128), 1)).astype(F32).astype(BF16)
    turned = nt(same, jnp.concatenate([two[...]] * 4, axis=0))
    off = iota((C2, 256), 1) >> 6
    wide = []
    for x in range(4):
        for y in range(4):
            e = 2 * (y & 1) + (x & 1)
            wide.append(jnp.where(off == 2 * (y >> 1) + (x >> 1), turned[e * C2 : (e + 1) * C2], 0.0))
    wide = jnp.concatenate(wide, axis=0).astype(BF16)
    one_t = one[...].astype(F32).T.astype(BF16)

    def block(i, carry):
        start = pl.multiple_of(i * BLOCK, BLOCK)
        first_up = nt(one_t, emb[pl.ds(start, BLOCK), :])
        parts = []
        for o in range(4):
            v = first_up[o * C1 : (o + 1) * C1, :]
            v = v - jnp.mean(v, axis=0, keepdims=True)
            v = v * lax.rsqrt(jnp.mean(v * v, axis=0, keepdims=True) + 1e-06)
            parts.append(gelu(v).astype(BF16))
        active = jnp.concatenate(parts, axis=0)
        up_ref[:, pl.ds(start, BLOCK)] = gelu(nn(wide, active)).astype(BF16)
        return carry

    ahead = iota((EW, 256), 1) - 4 * iota((EW, 256), 0)
    for x in range(4):
        lanes = (ahead == x).astype(F32).astype(BF16)
        spread_ref[x * 128 : x * 128 + 64, :] = lanes
        spread_ref[x * 128 + 64 : x * 128 + 128, :] = lanes
    lax.fori_loop(0, CELLS // BLOCK, block, 0, unroll=UNROLL)


def gathered_in(refs, bufs, sems):
    copies = [pltpu.make_async_copy(r, b, sems.at[i]) for i, (r, b) in enumerate(zip(refs, bufs))]
    for c in copies:
        c.start()
    for c in copies:
        c.wait()


def in_vmem(value):
    return pltpu.with_memory_space_constraint(value, pltpu.VMEM)


def is_early():
    return lax.axis_index("z") <= 7


def slots_kernel(early, tile, row, col, pts, conf, *rest):
    weights, (send, *tables), scratch = rest[:8], rest[8:12], rest[12:]
    bufs, sems = scratch[:8], scratch[8]
    t = tile[...]
    names = (iota((P_DEV, P_DEV), 0) == t).astype(F32)
    before = (iota((P_DEV, P_DEV), 0) < iota((P_DEV, P_DEV), 1)).astype(BF16)
    count = nn(names.astype(BF16), before)
    rank = jnp.sum(names * count, axis=0, keepdims=True).astype(I32)
    values = [row[...], col[...], conf[...], pts[0:1, :], pts[1:2, :]]
    group = iota((16, P_DEV), 0)
    x_of, s_of = group >> 2, group & 3
    dest = iota((NZ * NC, P_DEV), 0)

    def part(target, rank_at, values):
        mask = ((target >> 5) == x_of) & (rank_at == s_of)
        rows = [jnp.where(mask, v.astype(F32), 0.0) for v in values]
        rows += [jnp.zeros((16, P_DEV), F32)] * 3
        z, c = (target >> 1) - Z_FIRST, target - C_FIRST
        place = 2 * (z & 15) + (c & 1)
        return nt((place == dest).astype(BF16), jnp.concatenate(rows, axis=0).astype(BF16))

    out = part(t, rank, values) + part(t + 1, rank + 2, [values[0] - ROWS_T] + values[1:])
    send[...] = out.reshape(NZ * NC, 1, 128)

    @pl.when(early[0] == 1)
    def _():
        gathered_in(weights, bufs, sems)
        local_tables(*bufs, *tables)


def regroup_kernel(early, got, up_in, head_in, spread_in, *rest):
    weights, (send, *tables), scratch = rest[:8], rest[8:12], rest[12:]
    bufs, sems = scratch[:8], scratch[8]
    r = got[...].reshape(NZ * NC, 128)
    r = jnp.concatenate([r] * 4, axis=0)
    keep = (iota((128, 128), 1) & 3) == (iota((128, 128), 0) >> 5)
    r = jnp.where(keep, r, 0.0).astype(BF16)
    at, lane = iota((32, 128), 0), iota((32, 128), 1)
    pick = ((lane >> 4) == (at & 7)) & (((lane >> 2) & 3) == (at >> 3))
    out = nt(pick.astype(BF16), r)
    for i in range(NX):
        x = (X_FIRST + i) % NX
        for j in range(NR):
            send[i * NR + j] = out[x * 8 : (x + 1) * 8, :].astype(BF16)

    @pl.when(early[0] != 1)
    def _():
        gathered_in(weights, bufs, sems)
        local_tables(*bufs, *tables)


def mask_kernel(got, up, head, spread, out):
    lane = iota((8, 128), 1)
    own, below = [], []
    for j in range(8):
        a, b = got[j].astype(F32), got[j + 8].astype(F32)
        own.append(jnp.where(lane < 64, a, pltpu.roll(b, 64, 1)))
        below.append(jnp.where(lane < 64, pltpu.roll(a, 64, 1), b))
    own, below = (jnp.concatenate(v, axis=1).astype(BF16) for v in (own, below))
    many = 1024
    c_at = iota((EW, many), 0).astype(F32).astype(BF16)
    r_at = c_at[:16]
    zero, unit = BF16(0.0), BF16(1.0)
    blank = jnp.zeros((EW, many), BF16)

    def one_hot(v, at):
        return jnp.maximum(unit - jnp.abs(at - v), zero)

    def window(v, at):
        return jnp.clip(BF16(2.5) - jnp.abs(at - (v + BF16(1.5))), zero, unit)

    def factors(v, rows):
        row, col, conf, first, second = (v[i : i + 1, :] for i in range(5))
        ahead = r_at - (BF16(16.0) * first + second)
        hot = [jnp.where(ahead == BF16(-16.0 * i), unit, zero) for i in range(16)]
        hot = jnp.concatenate(hot, axis=0)
        heads = nn(head[...], hot).astype(BF16)
        in_row, in_col = window(row, r_at), window(col, c_at) * conf
        even, odd = jnp.concatenate([in_col, blank], axis=0), jnp.concatenate([blank, in_col], axis=0)
        lefts = [heads * in_row[i : i + 1, :] for i in range(rows)]
        return (
            nt(jnp.concatenate(lefts[0::2], axis=0), even)
            + nt(jnp.concatenate(lefts[1::2], axis=0), odd)
        )

    total = factors(own, 16)
    total = jnp.concatenate([total[:64] + factors(below, 4), total[64:]], axis=0)
    total = (total * 0.25).astype(BF16)

    at, lane = iota((32, 256), 0), iota((32, 256), 1)
    gather = ((lane >> 4) == 4 * (at >> 3) + (at & 3)).astype(F32).astype(BF16)
    mine = (iota((32, 256), 0) >> 2 & 1) == (iota((32, 256), 1) >> 6 & 1)
    blocks = []
    for j in range(0, 8, 2):
        cells = slice(j * 128, (j + 2) * 128)
        h = jnp.concatenate([total[(j + i) * 32 : (j + i + 1) * 32, :] for i in range(2)], axis=1)
        terms = [up[q * C2 : (q + 1) * C2, cells] * h for q in range(16)]
        terms = [t[:16] + t[16:] for t in terms]
        sums = jnp.where(mine, nn(gather, jnp.concatenate(terms, axis=0)), 0.0)
        for i in range(2):
            part = sums[:, i * 128 : (i + 1) * 128]
            blocks.append(jnp.concatenate([part[8 * x : 8 * x + 8] for x in range(NX)], axis=1))
    flat = jnp.concatenate(blocks, axis=0)
    top = flat.astype(BF16)
    rest = (flat - top.astype(F32)).astype(BF16)
    both = nn(jnp.concatenate([top, rest], axis=0), spread[...])
    out[...] = both[:64] + both[64:]


def on_device(
    embedding,
    prompt_tile,
    crop_row,
    crop_col,
    points,
    confidence,
    pe_matrix,
    point_embed,
    w_one,
    w_two,
    w_three,
    conv_one,
    conv_two,
):
    early = is_early().astype(I32).reshape(1)
    smem = pl.BlockSpec(memory_space=pltpu.SMEM)
    vmem = pl.BlockSpec(memory_space=pltpu.VMEM)
    hbm = pl.BlockSpec(memory_space=pl.ANY)
    weights = (
        embedding.reshape(CELLS, C),
        conv_one,
        conv_two,
        pe_matrix,
        point_embed.reshape(1, 256),
        w_one,
        w_two,
        w_three.T,
    )
    up_shape = pltpu.VMEM((16 * C2, CELLS), BF16)
    head_shape = pltpu.VMEM((C2, 256), BF16)
    tables = (up_shape, head_shape, pltpu.VMEM((512, 256), BF16))
    scratch = [pltpu.VMEM(w.shape, w.dtype) for w in weights] + [pltpu.SemaphoreType.DMA((8,))]
    send, *made = pl.pallas_call(
        slots_kernel,
        out_shape=(pltpu.VMEM((NZ * NC, 1, 128), F32), *tables),
        in_specs=[smem] + [vmem] * 5 + [hbm] * 8,
        out_specs=(vmem,) * 4,
        scratch_shapes=scratch,
    )(
        early,
        prompt_tile.reshape(1, P_DEV),
        crop_row.reshape(1, P_DEV),
        crop_col.reshape(1, P_DEV),
        points.T,
        confidence.reshape(1, P_DEV),
        *weights,
    )
    got = exchanged(send, column_groups())
    send, *made = pl.pallas_call(
        regroup_kernel,
        out_shape=(pltpu.VMEM((NX * NR, 8, 128), BF16), *tables),
        in_specs=[smem] + [vmem] * 4 + [hbm] * 8,
        out_specs=(vmem,) * 4,
        scratch_shapes=scratch,
        input_output_aliases={2: 1, 3: 2, 4: 3},
    )(early, in_vmem(got), *map(in_vmem, made), *weights)
    got = exchanged(send, plane_groups())
    return pl.pallas_call(
        mask_kernel,
        out_shape=jax.ShapeDtypeStruct((4 * ROWS_T, 4 * EW), F32),
        in_specs=[vmem] * 4,
        out_specs=vmem,
    )(in_vmem(got), *map(in_vmem, made))


def solution(mesh):
    split = Mesh(mesh.devices.reshape(NX, NZ, NC, NR), EVERY)
    tile, every = EVERY[:3], EVERY
    return jax.shard_map(
        on_device,
        mesh=split,
        in_specs=(
            P(tile, None, None),
            P(every, None),
            P(every),
            P(every),
            P(every, None),
            P(every),
            P(),
            P(),
            P(),
            P(),
            P(),
            P(),
            P(),
        ),
        out_specs=P(tile, None),
        check_vma=False,
    )
```

```python
import math

import jax
import jax.numpy as jnp
from jax import lax
from jax.experimental import pallas as pl
from jax.experimental.pallas import tpu as pltpu
from jax.sharding import Mesh
from jax.sharding import PartitionSpec as P

CK = 4
C = 256
C1 = 64
C2 = 32
ROWS_T = 16
EW = 64
P_DEV = 128
NX, NZ, NC, NR = 4, 16, 2, 4
CELLS = ROWS_T * EW
Z_FIRST, C_FIRST, X_FIRST, R_FIRST = 8, 1, 2, 2
UNROLL, BLOCK = 4, 256
EVERY = ("x", "z", "core", "rep")
F32 = jnp.float32
BF16 = jnp.bfloat16
I32 = jnp.int32


def iota(shape, dim):
    return lax.broadcasted_iota(I32, shape, dim)


def flat(x, z, c, r):
    return ((x % NX * NZ + z % NZ) * NC + c % NC) * NR + r % NR


def exchanged(value, groups):
    return lax.all_to_all(value, EVERY, 0, 0, axis_index_groups=groups, tiled=True)


def column_groups():
    return [
        [flat(x, Z_FIRST + i, C_FIRST + j, r) for i in range(NZ) for j in range(NC)]
        for x in range(NX)
        for r in range(NR)
    ]


def plane_groups():
    return [
        [flat(X_FIRST + i, z, c, R_FIRST + j) for i in range(NX) for j in range(NR)]
        for z in range(NZ)
        for c in range(NC)
    ]


def nt(a, b):
    return lax.dot_general(a, b, (((1,), (1,)), ((), ())), preferred_element_type=F32)


def nn(a, b):
    return jnp.dot(a, b, preferred_element_type=F32)


def gelu(v):
    return 0.5 * v * (1.0 + lax.erf(v * (1.0 / math.sqrt(2.0))))


def local_tables(emb, one, two, pe, bias, w1, w2, w3, up_ref, head_ref, spread_ref):
    coord = (iota((16, P_DEV), 0).astype(F32) + 0.5) / (4.0 * CK) * 2.0 - 1.0
    angle_a = coord * pe[0:1, :] * (2.0 * math.pi)
    angle_b = coord * pe[1:2, :] * (2.0 * math.pi)
    sin_a, cos_a, sin_b, cos_b = jnp.sin(angle_a), jnp.cos(angle_a), jnp.sin(angle_b), jnp.cos(angle_b)
    sines, cosines = [], []
    for i in range(16):
        sin_i, cos_i = sin_a[i : i + 1, :], cos_a[i : i + 1, :]
        sines.append(sin_i * cos_b + cos_i * sin_b)
        cosines.append(cos_i * cos_b - sin_i * sin_b)
    sines, cosines = jnp.concatenate(sines, axis=0), jnp.concatenate(cosines, axis=0)
    tokens = (jnp.concatenate([sines, cosines], axis=1) + bias[...]).astype(BF16)
    hidden = jnp.maximum(nn(tokens, w1[...]), 0.0).astype(BF16)
    hidden = jnp.maximum(nn(hidden, w2[...]), 0.0).astype(BF16)
    head_ref[...] = nt(w3[...], hidden).astype(BF16)

    row = iota((16, P_DEV), 0)
    x, y = row >> 2, row & 3
    ahead = iota((16, P_DEV), 1) - (2 * (y & 1) + (x & 1)) * C2
    pick = jnp.concatenate([(ahead == k).astype(F32) for k in range(C2)], axis=0).astype(BF16)
    row = iota((16, 256), 0)
    keep = (iota((16, 256), 1) >> 6) == 2 * ((row & 3) >> 1) + (row >> 3)
    spread = nt(pick, jnp.concatenate([two[...]] * 4, axis=0))
    wide = [jnp.where(keep, spread[16 * k : 16 * k + 16], 0.0) for k in range(C2)]
    wide = jnp.concatenate(wide, axis=0).astype(BF16)
    one_t = one[...].astype(F32).T.astype(BF16)

    def block(i, carry):
        start = pl.multiple_of(i * BLOCK, BLOCK)
        first_up = nt(one_t, emb[pl.ds(start, BLOCK), :])
        parts = []
        for o in range(4):
            v = first_up[o * C1 : (o + 1) * C1, :]
            v = v - jnp.mean(v, axis=0, keepdims=True)
            v = v * lax.rsqrt(jnp.mean(v * v, axis=0, keepdims=True) + 1e-06)
            parts.append(gelu(v).astype(BF16))
        active = jnp.concatenate(parts, axis=0)
        up_ref[:, pl.ds(start, BLOCK)] = gelu(nn(wide, active)).astype(BF16)
        return carry

    ahead = iota((EW, 256), 1) - 4 * iota((EW, 256), 0)
    for x in range(4):
        lanes = (ahead == x).astype(F32).astype(BF16)
        spread_ref[x * 128 : x * 128 + 64, :] = lanes
        spread_ref[x * 128 + 64 : x * 128 + 128, :] = lanes
    lax.fori_loop(0, CELLS // BLOCK, block, 0, unroll=UNROLL)


def gathered_in(refs, bufs, sems):
    copies = [pltpu.make_async_copy(r, b, sems.at[i]) for i, (r, b) in enumerate(zip(refs, bufs))]
    for c in copies:
        c.start()
    for c in copies:
        c.wait()


def in_vmem(value):
    return pltpu.with_memory_space_constraint(value, pltpu.VMEM)


def is_early():
    return lax.axis_index("z") <= 7


def slots_kernel(early, tile, row, col, pts, conf, *rest):
    weights, (send, *tables), scratch = rest[:8], rest[8:12], rest[12:]
    bufs, sems = scratch[:8], scratch[8]
    t = tile[...]
    names = (iota((P_DEV, P_DEV), 0) == t).astype(F32)
    before = (iota((P_DEV, P_DEV), 0) < iota((P_DEV, P_DEV), 1)).astype(BF16)
    count = nn(names.astype(BF16), before)
    rank = jnp.sum(names * count, axis=0, keepdims=True).astype(I32)
    values = [row[...], col[...], conf[...], pts[0:1, :], pts[1:2, :]]
    group = iota((16, P_DEV), 0)
    x_of, s_of = group >> 2, group & 3
    dest = iota((NZ * NC, P_DEV), 0)

    def part(target, rank_at, values):
        mask = ((target >> 5) == x_of) & (rank_at == s_of)
        rows = [jnp.where(mask, v.astype(F32), 0.0) for v in values]
        rows += [jnp.zeros((16, P_DEV), F32)] * 3
        z, c = (target >> 1) - Z_FIRST, target - C_FIRST
        place = 2 * (z & 15) + (c & 1)
        return nt((place == dest).astype(BF16), jnp.concatenate(rows, axis=0).astype(BF16))

    out = part(t, rank, values) + part(t + 1, rank + 2, [values[0] - ROWS_T] + values[1:])
    send[...] = out.reshape(NZ * NC, 1, 128)

    @pl.when(early[0] == 1)
    def _():
        gathered_in(weights, bufs, sems)
        local_tables(*bufs, *tables)


def regroup_kernel(early, got, up_in, head_in, spread_in, *rest):
    weights, (send, *tables), scratch = rest[:8], rest[8:12], rest[12:]
    bufs, sems = scratch[:8], scratch[8]
    r = got[...].reshape(NZ * NC, 128)
    r = jnp.concatenate([r] * 4, axis=0)
    keep = (iota((128, 128), 1) & 3) == (iota((128, 128), 0) >> 5)
    r = jnp.where(keep, r, 0.0).astype(BF16)
    at, lane = iota((32, 128), 0), iota((32, 128), 1)
    pick = ((lane >> 4) == (at & 7)) & (((lane >> 2) & 3) == (at >> 3))
    out = nt(pick.astype(BF16), r)
    for i in range(NX):
        x = (X_FIRST + i) % NX
        for j in range(NR):
            send[i * NR + j] = out[x * 8 : (x + 1) * 8, :].astype(BF16)

    @pl.when(early[0] != 1)
    def _():
        gathered_in(weights, bufs, sems)
        local_tables(*bufs, *tables)


def mask_kernel(got, up, head, spread, out):
    lane = iota((8, 128), 1)
    own, below = [], []
    for j in range(8):
        a, b = got[j].astype(F32), got[j + 8].astype(F32)
        own.append(jnp.where(lane < 64, a, pltpu.roll(b, 64, 1)))
        below.append(jnp.where(lane < 64, pltpu.roll(a, 64, 1), b))
    own, below = (jnp.concatenate(v, axis=1).astype(BF16) for v in (own, below))
    many = 1024
    c_at = iota((EW, many), 0).astype(F32).astype(BF16)
    r_at = c_at[:16]
    zero, unit = BF16(0.0), BF16(1.0)
    left = iota((C2, 128), 1) < 64

    def window(v, at):
        return jnp.clip(BF16(2.5) - jnp.abs(at - (v + BF16(1.5))), zero, unit)

    def factors(v, rows):
        row, col, conf, first, second = (v[i : i + 1, :] for i in range(5))
        ahead = r_at - (BF16(16.0) * first + second)
        hot = [jnp.where(ahead == BF16(-16.0 * i), unit, zero) for i in range(16)]
        hot = jnp.concatenate(hot, axis=0)
        heads = nn(head[...], hot).astype(BF16)
        in_row, in_col = window(row, r_at), window(col, c_at) * conf
        in_col = jnp.concatenate([in_col, in_col], axis=0)
        lefts = [heads * in_row[i : i + 1, :] for i in range(rows)]
        half = max(rows // 2, 4)
        sums = [nt(jnp.concatenate(lefts[i : i + half], axis=0), in_col) for i in range(0, rows, half)]
        sums = jnp.concatenate(sums, axis=0)
        sums = [jnp.where(left, sums[i : i + 32], sums[i + 32 : i + 64]) for i in range(0, 32 * rows, 64)]
        return jnp.concatenate(sums, axis=0)

    total = factors(own, 16)
    total = jnp.concatenate([total[:64] + factors(below, 4), total[64:]], axis=0)
    total = total * 0.25

    sub = iota((8, 128), 0)
    mine = (sub >> 2) == (iota((8, 128), 1) >> 6)
    blocks = []
    for j in range(8):
        cells = slice(j * 128, (j + 1) * 128)
        h = total[j * 32 : (j + 1) * 32, :]
        terms = [up[k * 16 : (k + 1) * 16, cells].astype(F32) * h[k : k + 1, :] for k in range(C2)]
        while len(terms) > 1:
            terms = [a + b for a, b in zip(terms[0::2], terms[1::2])]
        pieces = []
        for v in (terms[0][:8], terms[0][8:]):
            turned = pltpu.roll(v, 4, 0)
            pieces.append(jnp.where(mine, jnp.where(sub < 4, v, turned), 0.0))
            pieces.append(jnp.where(mine, jnp.where(sub < 4, turned, v), 0.0))
        blocks.append(jnp.concatenate(pieces, axis=1))
    flat = jnp.concatenate(blocks, axis=0)
    top = flat.astype(BF16)
    rest = (flat - top.astype(F32)).astype(BF16)
    both = nn(jnp.concatenate([top, rest], axis=0), spread[...])
    out[...] = both[:64] + both[64:]


def on_device(
    embedding,
    prompt_tile,
    crop_row,
    crop_col,
    points,
    confidence,
    pe_matrix,
    point_embed,
    w_one,
    w_two,
    w_three,
    conv_one,
    conv_two,
):
    early = is_early().astype(I32).reshape(1)
    smem = pl.BlockSpec(memory_space=pltpu.SMEM)
    vmem = pl.BlockSpec(memory_space=pltpu.VMEM)
    hbm = pl.BlockSpec(memory_space=pl.ANY)
    weights = (
        embedding.reshape(CELLS, C),
        conv_one,
        conv_two,
        pe_matrix,
        point_embed.reshape(1, 256),
        w_one,
        w_two,
        w_three.T,
    )
    up_shape = pltpu.VMEM((16 * C2, CELLS), BF16)
    head_shape = pltpu.VMEM((C2, 256), BF16)
    tables = (up_shape, head_shape, pltpu.VMEM((512, 256), BF16))
    scratch = [pltpu.VMEM(w.shape, w.dtype) for w in weights] + [pltpu.SemaphoreType.DMA((8,))]
    send, *made = pl.pallas_call(
        slots_kernel,
        out_shape=(pltpu.VMEM((NZ * NC, 1, 128), F32), *tables),
        in_specs=[smem] + [vmem] * 5 + [hbm] * 8,
        out_specs=(vmem,) * 4,
        scratch_shapes=scratch,
    )(
        early,
        prompt_tile.reshape(1, P_DEV),
        crop_row.reshape(1, P_DEV),
        crop_col.reshape(1, P_DEV),
        points.T,
        confidence.reshape(1, P_DEV),
        *weights,
    )
    got = exchanged(send, column_groups())
    send, *made = pl.pallas_call(
        regroup_kernel,
        out_shape=(pltpu.VMEM((NX * NR, 8, 128), BF16), *tables),
        in_specs=[smem] + [vmem] * 4 + [hbm] * 8,
        out_specs=(vmem,) * 4,
        scratch_shapes=scratch,
        input_output_aliases={2: 1, 3: 2, 4: 3},
    )(early, in_vmem(got), *map(in_vmem, made), *weights)
    got = exchanged(send, plane_groups())
    return pl.pallas_call(
        mask_kernel,
        out_shape=jax.ShapeDtypeStruct((4 * ROWS_T, 4 * EW), F32),
        in_specs=[vmem] * 4,
        out_specs=vmem,
    )(in_vmem(got), *map(in_vmem, made))


def solution(mesh):
    split = Mesh(mesh.devices.reshape(NX, NZ, NC, NR), EVERY)
    tile, every = EVERY[:3], EVERY
    return jax.shard_map(
        on_device,
        mesh=split,
        in_specs=(
            P(tile, None, None),
            P(every, None),
            P(every),
            P(every),
            P(every, None),
            P(every),
            P(),
            P(),
            P(),
            P(),
            P(),
            P(),
            P(),
        ),
        out_specs=P(tile, None),
        check_vma=False,
    )
```

```python
import math

import jax
import jax.numpy as jnp
from jax import lax
from jax.experimental import pallas as pl
from jax.experimental.pallas import tpu as pltpu
from jax.sharding import Mesh
from jax.sharding import PartitionSpec as P

CK = 4
C = 256
C1 = 64
C2 = 32
ROWS_T = 16
EW = 64
P_DEV = 128
NX, NZ, NC, NR = 4, 16, 2, 4
CELLS = ROWS_T * EW
Z_FIRST, C_FIRST, X_FIRST, R_FIRST = 9, 1, 2, 2
UNROLL, BLOCK = 4, 256
EVERY = ("x", "z", "core", "rep")
F32 = jnp.float32
BF16 = jnp.bfloat16
I32 = jnp.int32


def iota(shape, dim):
    return lax.broadcasted_iota(I32, shape, dim)


def flat(x, z, c, r):
    return ((x % NX * NZ + z % NZ) * NC + c % NC) * NR + r % NR


def exchanged(value, groups):
    return lax.all_to_all(value, EVERY, 0, 0, axis_index_groups=groups, tiled=True)


def column_groups():
    return [
        [flat(x, Z_FIRST + i, C_FIRST + j, r) for i in range(NZ) for j in range(NC)]
        for x in range(NX)
        for r in range(NR)
    ]


def plane_groups():
    return [
        [flat(X_FIRST + i, z, c, R_FIRST + j) for i in range(NX) for j in range(NR)]
        for z in range(NZ)
        for c in range(NC)
    ]


def nt(a, b):
    return lax.dot_general(a, b, (((1,), (1,)), ((), ())), preferred_element_type=F32)


def nn(a, b):
    return jnp.dot(a, b, preferred_element_type=F32)


def gelu(v):
    return 0.5 * v * (1.0 + lax.erf(v * (1.0 / math.sqrt(2.0))))


def local_tables(emb, one, two, pe, bias, w1, w2, w3, up_ref, head_ref, spread_ref):
    coord = (iota((16, P_DEV), 0).astype(F32) + 0.5) / (4.0 * CK) * 2.0 - 1.0
    angle_a = coord * pe[0:1, :] * (2.0 * math.pi)
    angle_b = coord * pe[1:2, :] * (2.0 * math.pi)
    sin_a, cos_a, sin_b, cos_b = jnp.sin(angle_a), jnp.cos(angle_a), jnp.sin(angle_b), jnp.cos(angle_b)
    sines, cosines = [], []
    for i in range(16):
        sin_i, cos_i = sin_a[i : i + 1, :], cos_a[i : i + 1, :]
        sines.append(sin_i * cos_b + cos_i * sin_b)
        cosines.append(cos_i * cos_b - sin_i * sin_b)
    sines, cosines = jnp.concatenate(sines, axis=0), jnp.concatenate(cosines, axis=0)
    tokens = (jnp.concatenate([sines, cosines], axis=1) + bias[...]).astype(BF16)
    hidden = jnp.maximum(nn(tokens, w1[...]), 0.0).astype(BF16)
    hidden = jnp.maximum(nn(hidden, w2[...]), 0.0).astype(BF16)
    head_ref[...] = nt(w3[...], hidden).astype(BF16)

    row = iota((16, P_DEV), 0)
    x, y = row >> 2, row & 3
    ahead = iota((16, P_DEV), 1) - (2 * (y & 1) + (x & 1)) * C2
    pick = jnp.concatenate([(ahead == k).astype(F32) for k in range(C2)], axis=0).astype(BF16)
    row = iota((16, 256), 0)
    keep = (iota((16, 256), 1) >> 6) == 2 * ((row & 3) >> 1) + (row >> 3)
    spread = nt(pick, jnp.concatenate([two[...]] * 4, axis=0))
    wide = [jnp.where(keep, spread[16 * k : 16 * k + 16], 0.0) for k in range(C2)]
    wide = jnp.concatenate(wide, axis=0).astype(BF16)
    one_t = one[...].astype(F32).T.astype(BF16)

    def block(i, carry):
        start = pl.multiple_of(i * BLOCK, BLOCK)
        first_up = nt(one_t, emb[pl.ds(start, BLOCK), :])
        parts = []
        for o in range(4):
            v = first_up[o * C1 : (o + 1) * C1, :]
            v = v - jnp.mean(v, axis=0, keepdims=True)
            v = v * lax.rsqrt(jnp.mean(v * v, axis=0, keepdims=True) + 1e-06)
            parts.append(gelu(v).astype(BF16))
        active = jnp.concatenate(parts, axis=0)
        up_ref[:, pl.ds(start, BLOCK)] = gelu(nn(wide, active)).astype(BF16)
        return carry

    ahead = iota((EW, 256), 1) - 4 * iota((EW, 256), 0)
    for x in range(4):
        lanes = (ahead == x).astype(F32).astype(BF16)
        spread_ref[x * 128 : x * 128 + 64, :] = lanes
        spread_ref[x * 128 + 64 : x * 128 + 128, :] = lanes
    lax.fori_loop(0, CELLS // BLOCK, block, 0, unroll=UNROLL)


def gathered_in(refs, bufs, sems):
    copies = [pltpu.make_async_copy(r, b, sems.at[i]) for i, (r, b) in enumerate(zip(refs, bufs))]
    for c in copies:
        c.start()
    for c in copies:
        c.wait()


def in_vmem(value):
    return pltpu.with_memory_space_constraint(value, pltpu.VMEM)


def is_early():
    return lax.axis_index("z") <= 7


def slots_kernel(early, tile, row, col, pts, conf, *rest):
    weights, (send, *tables), scratch = rest[:8], rest[8:12], rest[12:]
    bufs, sems = scratch[:8], scratch[8]
    t = tile[...]
    names = (iota((P_DEV, P_DEV), 0) == t).astype(F32)
    before = (iota((P_DEV, P_DEV), 0) < iota((P_DEV, P_DEV), 1)).astype(BF16)
    count = nn(names.astype(BF16), before)
    rank = jnp.sum(names * count, axis=0, keepdims=True).astype(I32)
    values = [row[...], col[...], conf[...], pts[0:1, :], pts[1:2, :]]
    group = iota((16, P_DEV), 0)
    x_of, s_of = group >> 2, group & 3
    dest = iota((NZ * NC, P_DEV), 0)

    def part(target, rank_at, values):
        mask = ((target >> 5) == x_of) & (rank_at == s_of)
        rows = [jnp.where(mask, v.astype(F32), 0.0) for v in values]
        rows += [jnp.zeros((16, P_DEV), F32)] * 3
        z, c = (target >> 1) - Z_FIRST, target - C_FIRST
        place = 2 * (z & 15) + (c & 1)
        return nt((place == dest).astype(BF16), jnp.concatenate(rows, axis=0).astype(BF16))

    out = part(t, rank, values) + part(t + 1, rank + 2, [values[0] - ROWS_T] + values[1:])
    send[...] = out.reshape(NZ * NC, 1, 128)

    @pl.when(early[0] == 1)
    def _():
        gathered_in(weights, bufs, sems)
        local_tables(*bufs, *tables)


def regroup_kernel(early, got, up_in, head_in, spread_in, *rest):
    weights, (send, *tables), scratch = rest[:8], rest[8:12], rest[12:]
    bufs, sems = scratch[:8], scratch[8]
    r = got[...].reshape(NZ * NC, 128)
    r = jnp.concatenate([r] * 4, axis=0)
    keep = (iota((128, 128), 1) & 3) == (iota((128, 128), 0) >> 5)
    r = jnp.where(keep, r, 0.0).astype(BF16)
    at, lane = iota((32, 128), 0), iota((32, 128), 1)
    pick = ((lane >> 4) == (at & 7)) & (((lane >> 2) & 3) == (at >> 3))
    out = nt(pick.astype(BF16), r)
    for i in range(NX):
        x = (X_FIRST + i) % NX
        for j in range(NR):
            send[i * NR + j] = out[x * 8 : (x + 1) * 8, :].astype(BF16)

    @pl.when(early[0] != 1)
    def _():
        gathered_in(weights, bufs, sems)
        local_tables(*bufs, *tables)


def mask_kernel(got, up, head, spread, out):
    lane = iota((8, 128), 1)
    own, below = [], []
    for j in range(8):
        a, b = got[j].astype(F32), got[j + 8].astype(F32)
        own.append(jnp.where(lane < 64, a, pltpu.roll(b, 64, 1)))
        below.append(jnp.where(lane < 64, pltpu.roll(a, 64, 1), b))
    own, below = (jnp.concatenate(v, axis=1).astype(BF16) for v in (own, below))
    many = 1024
    c_at = iota((EW, many), 0).astype(F32).astype(BF16)
    r_at = c_at[:16]
    zero, unit = BF16(0.0), BF16(1.0)
    left = iota((C2, 128), 1) < 64

    def window(v, at):
        return jnp.clip(BF16(2.5) - jnp.abs(at - (v + BF16(1.5))), zero, unit)

    def factors(v, rows):
        row, col, conf, first, second = (v[i : i + 1, :] for i in range(5))
        ahead = r_at - (BF16(16.0) * first + second)
        hot = [jnp.where(ahead == BF16(-16.0 * i), unit, zero) for i in range(16)]
        hot = jnp.concatenate(hot, axis=0)
        heads = nn(head[...], hot).astype(BF16)
        in_row, in_col = window(row, r_at), window(col, c_at) * conf
        in_col = jnp.concatenate([in_col, in_col], axis=0)
        lefts = [heads * in_row[i : i + 1, :] for i in range(rows)]
        half = max(rows // 2, 4)
        sums = [nt(jnp.concatenate(lefts[i : i + half], axis=0), in_col) for i in range(0, rows, half)]
        sums = jnp.concatenate(sums, axis=0)
        sums = [jnp.where(left, sums[i : i + 32], sums[i + 32 : i + 64]) for i in range(0, 32 * rows, 64)]
        return jnp.concatenate(sums, axis=0)

    total = factors(own, 16)
    total = jnp.concatenate([total[:64] + factors(below, 4), total[64:]], axis=0)
    total = total * 0.25

    sub = iota((8, 128), 0)
    mine = (sub >> 2) == (iota((8, 128), 1) >> 6)
    blocks = []
    for j in range(8):
        cells = slice(j * 128, (j + 1) * 128)
        h = total[j * 32 : (j + 1) * 32, :]
        terms = [up[k * 16 : (k + 1) * 16, cells].astype(F32) * h[k : k + 1, :] for k in range(C2)]
        while len(terms) > 1:
            terms = [a + b for a, b in zip(terms[0::2], terms[1::2])]
        pieces = []
        for v in (terms[0][:8], terms[0][8:]):
            turned = pltpu.roll(v, 4, 0)
            pieces.append(jnp.where(mine, jnp.where(sub < 4, v, turned), 0.0))
            pieces.append(jnp.where(mine, jnp.where(sub < 4, turned, v), 0.0))
        blocks.append(jnp.concatenate(pieces, axis=1))
    flat = jnp.concatenate(blocks, axis=0)
    top = flat.astype(BF16)
    rest = (flat - top.astype(F32)).astype(BF16)
    both = nn(jnp.concatenate([top, rest], axis=0), spread[...])
    out[...] = both[:64] + both[64:]


def on_device(
    embedding,
    prompt_tile,
    crop_row,
    crop_col,
    points,
    confidence,
    pe_matrix,
    point_embed,
    w_one,
    w_two,
    w_three,
    conv_one,
    conv_two,
):
    early = is_early().astype(I32).reshape(1)
    smem = pl.BlockSpec(memory_space=pltpu.SMEM)
    vmem = pl.BlockSpec(memory_space=pltpu.VMEM)
    hbm = pl.BlockSpec(memory_space=pl.ANY)
    weights = (
        embedding.reshape(CELLS, C),
        conv_one,
        conv_two,
        pe_matrix,
        point_embed.reshape(1, 256),
        w_one,
        w_two,
        w_three.T,
    )
    up_shape = pltpu.VMEM((16 * C2, CELLS), BF16)
    head_shape = pltpu.VMEM((C2, 256), BF16)
    tables = (up_shape, head_shape, pltpu.VMEM((512, 256), BF16))
    scratch = [pltpu.VMEM(w.shape, w.dtype) for w in weights] + [pltpu.SemaphoreType.DMA((8,))]
    send, *made = pl.pallas_call(
        slots_kernel,
        out_shape=(pltpu.VMEM((NZ * NC, 1, 128), F32), *tables),
        in_specs=[smem] + [vmem] * 5 + [hbm] * 8,
        out_specs=(vmem,) * 4,
        scratch_shapes=scratch,
    )(
        early,
        prompt_tile.reshape(1, P_DEV),
        crop_row.reshape(1, P_DEV),
        crop_col.reshape(1, P_DEV),
        points.T,
        confidence.reshape(1, P_DEV),
        *weights,
    )
    got = exchanged(send, column_groups())
    send, *made = pl.pallas_call(
        regroup_kernel,
        out_shape=(pltpu.VMEM((NX * NR, 8, 128), BF16), *tables),
        in_specs=[smem] + [vmem] * 4 + [hbm] * 8,
        out_specs=(vmem,) * 4,
        scratch_shapes=scratch,
        input_output_aliases={2: 1, 3: 2, 4: 3},
    )(early, in_vmem(got), *map(in_vmem, made), *weights)
    got = exchanged(send, plane_groups())
    return pl.pallas_call(
        mask_kernel,
        out_shape=jax.ShapeDtypeStruct((4 * ROWS_T, 4 * EW), F32),
        in_specs=[vmem] * 4,
        out_specs=vmem,
    )(in_vmem(got), *map(in_vmem, made))


def solution(mesh):
    split = Mesh(mesh.devices.reshape(NX, NZ, NC, NR), EVERY)
    tile, every = EVERY[:3], EVERY
    return jax.shard_map(
        on_device,
        mesh=split,
        in_specs=(
            P(tile, None, None),
            P(every, None),
            P(every),
            P(every),
            P(every, None),
            P(every),
            P(),
            P(),
            P(),
            P(),
            P(),
            P(),
            P(),
        ),
        out_specs=P(tile, None),
        check_vma=False,
    )
```

```python
import math

import jax
import jax.numpy as jnp
from jax import lax
from jax.experimental import pallas as pl
from jax.experimental.pallas import tpu as pltpu
from jax.sharding import Mesh
from jax.sharding import PartitionSpec as P

CK = 4
C = 256
C1 = 64
C2 = 32
ROWS_T = 16
EW = 64
P_DEV = 128
NX, NZ, NC, NR = 4, 16, 2, 4
CELLS = ROWS_T * EW
Z_FIRST, C_FIRST, X_FIRST, R_FIRST = 9, 1, 2, 2
UNROLL, BLOCK = 4, 256
EVERY = ("x", "z", "core", "rep")
F32 = jnp.float32
BF16 = jnp.bfloat16
I32 = jnp.int32


def iota(shape, dim):
    return lax.broadcasted_iota(I32, shape, dim)


def flat(x, z, c, r):
    return ((x % NX * NZ + z % NZ) * NC + c % NC) * NR + r % NR


def exchanged(value, groups):
    return lax.all_to_all(value, EVERY, 0, 0, axis_index_groups=groups, tiled=True)


def column_groups():
    return [
        [flat(x, Z_FIRST + i, C_FIRST + j, r) for i in range(NZ) for j in range(NC)]
        for x in range(NX)
        for r in range(NR)
    ]


def plane_groups():
    return [
        [flat(X_FIRST + i, z, c, R_FIRST + j) for i in range(NX) for j in range(NR)]
        for z in range(NZ)
        for c in range(NC)
    ]


def nt(a, b):
    return lax.dot_general(a, b, (((1,), (1,)), ((), ())), preferred_element_type=F32)


def nn(a, b):
    return jnp.dot(a, b, preferred_element_type=F32)


def gelu(v):
    return 0.5 * v * (1.0 + lax.erf(v * (1.0 / math.sqrt(2.0))))


def local_tables(emb, one, two, pe, bias, w1, w2, w3, up_ref, head_ref, spread_ref):
    coord = (iota((16, P_DEV), 0).astype(F32) + 0.5) / (4.0 * CK) * 2.0 - 1.0
    angle_a = coord * pe[0:1, :] * (2.0 * math.pi)
    angle_b = coord * pe[1:2, :] * (2.0 * math.pi)
    sin_a, cos_a, sin_b, cos_b = jnp.sin(angle_a), jnp.cos(angle_a), jnp.sin(angle_b), jnp.cos(angle_b)
    sines, cosines = [], []
    for i in range(16):
        sin_i, cos_i = sin_a[i : i + 1, :], cos_a[i : i + 1, :]
        sines.append(sin_i * cos_b + cos_i * sin_b)
        cosines.append(cos_i * cos_b - sin_i * sin_b)
    sines, cosines = jnp.concatenate(sines, axis=0), jnp.concatenate(cosines, axis=0)
    tokens = (jnp.concatenate([sines, cosines], axis=1) + bias[...]).astype(BF16)
    hidden = jnp.maximum(nn(tokens, w1[...]), 0.0).astype(BF16)
    hidden = jnp.maximum(nn(hidden, w2[...]), 0.0).astype(BF16)
    head_ref[...] = nt(w3[...], hidden).astype(BF16)

    row = iota((16, P_DEV), 0)
    x, y = row >> 2, row & 3
    ahead = iota((16, P_DEV), 1) - (2 * (y & 1) + (x & 1)) * C2
    pick = jnp.concatenate([(ahead == k).astype(F32) for k in range(C2)], axis=0).astype(BF16)
    row = iota((16, 256), 0)
    keep = (iota((16, 256), 1) >> 6) == 2 * ((row & 3) >> 1) + (row >> 3)
    spread = nt(pick, jnp.concatenate([two[...]] * 4, axis=0))
    wide = [jnp.where(keep, spread[16 * k : 16 * k + 16], 0.0) for k in range(C2)]
    wide = jnp.concatenate(wide, axis=0).astype(BF16)
    one_t = one[...].astype(F32).T.astype(BF16)

    def block(i, carry):
        start = pl.multiple_of(i * BLOCK, BLOCK)
        first_up = nt(one_t, emb[pl.ds(start, BLOCK), :])
        parts = []
        for o in range(4):
            v = first_up[o * C1 : (o + 1) * C1, :]
            v = v - jnp.mean(v, axis=0, keepdims=True)
            v = v * lax.rsqrt(jnp.mean(v * v, axis=0, keepdims=True) + 1e-06)
            parts.append(gelu(v).astype(BF16))
        active = jnp.concatenate(parts, axis=0)
        up_ref[:, pl.ds(start, BLOCK)] = gelu(nn(wide, active)).astype(BF16)
        return carry

    ahead = iota((EW, 256), 1) - 4 * iota((EW, 256), 0)
    for x in range(4):
        lanes = (ahead == x).astype(F32).astype(BF16)
        spread_ref[x * 128 : x * 128 + 64, :] = lanes
        spread_ref[x * 128 + 64 : x * 128 + 128, :] = lanes
    lax.fori_loop(0, CELLS // BLOCK, block, 0, unroll=UNROLL)


def gathered_in(refs, bufs, sems):
    copies = [pltpu.make_async_copy(r, b, sems.at[i]) for i, (r, b) in enumerate(zip(refs, bufs))]
    for c in copies:
        c.start()
    for c in copies:
        c.wait()


def in_vmem(value):
    return pltpu.with_memory_space_constraint(value, pltpu.VMEM)


def is_early():
    return lax.axis_index("z") <= 7


def slots_kernel(tile, row, col, pts, conf, *rest):
    weights, (send, *tables), scratch = rest[:8], rest[8:12], rest[12:]
    bufs, sems = scratch[:8], scratch[8]
    t = tile[...]
    names = (iota((P_DEV, P_DEV), 0) == t).astype(F32)
    before = (iota((P_DEV, P_DEV), 0) < iota((P_DEV, P_DEV), 1)).astype(BF16)
    count = nn(names.astype(BF16), before)
    rank = jnp.sum(names * count, axis=0, keepdims=True).astype(I32)
    values = [row[...], col[...], conf[...], pts[0:1, :], pts[1:2, :]]
    group = iota((16, P_DEV), 0)
    x_of, s_of = group >> 2, group & 3
    dest = iota((NZ * NC, P_DEV), 0)

    def part(target, rank_at, values):
        mask = ((target >> 5) == x_of) & (rank_at == s_of)
        rows = [jnp.where(mask, v.astype(F32), 0.0) for v in values]
        rows += [jnp.zeros((16, P_DEV), F32)] * 3
        z, c = (target >> 1) - Z_FIRST, target - C_FIRST
        place = 2 * (z & 15) + (c & 1)
        return nt((place == dest).astype(BF16), jnp.concatenate(rows, axis=0).astype(BF16))

    out = part(t, rank, values) + part(t + 1, rank + 2, [values[0] - ROWS_T] + values[1:])
    send[...] = out.reshape(NZ * NC, 1, 128)

    @pl.when(is_early())
    def _():
        gathered_in(weights, bufs, sems)
        local_tables(*bufs, *tables)


def regroup_kernel(got, up_in, head_in, spread_in, *rest):
    weights, (send, *tables), scratch = rest[:8], rest[8:12], rest[12:]
    bufs, sems = scratch[:8], scratch[8]
    r = got[...].reshape(NZ * NC, 128)
    r = jnp.concatenate([r] * 4, axis=0)
    keep = (iota((128, 128), 1) & 3) == (iota((128, 128), 0) >> 5)
    r = jnp.where(keep, r, 0.0).astype(BF16)
    at, lane = iota((32, 128), 0), iota((32, 128), 1)
    pick = ((lane >> 4) == (at & 7)) & (((lane >> 2) & 3) == (at >> 3))
    out = nt(pick.astype(BF16), r)
    for i in range(NX):
        x = (X_FIRST + i) % NX
        for j in range(NR):
            send[i * NR + j] = out[x * 8 : (x + 1) * 8, :].astype(BF16)

    @pl.when(jnp.logical_not(is_early()))
    def _():
        gathered_in(weights, bufs, sems)
        local_tables(*bufs, *tables)


def mask_kernel(got, up, head, spread, out):
    lane = iota((8, 128), 1)
    own, below = [], []
    for j in range(8):
        a, b = got[j].astype(F32), got[j + 8].astype(F32)
        own.append(jnp.where(lane < 64, a, pltpu.roll(b, 64, 1)))
        below.append(jnp.where(lane < 64, pltpu.roll(a, 64, 1), b))
    own, below = (jnp.concatenate(v, axis=1).astype(BF16) for v in (own, below))
    many = 1024
    c_at = iota((EW, many), 0).astype(F32).astype(BF16)
    r_at = c_at[:16]
    zero, unit = BF16(0.0), BF16(1.0)
    left = iota((C2, 128), 1) < 64

    def window(v, at):
        return jnp.clip(BF16(2.5) - jnp.abs(at - (v + BF16(1.5))), zero, unit)

    def factors(v, rows):
        row, col, conf, first, second = (v[i : i + 1, :] for i in range(5))
        ahead = r_at - (BF16(16.0) * first + second)
        hot = [jnp.where(ahead == BF16(-16.0 * i), unit, zero) for i in range(16)]
        hot = jnp.concatenate(hot, axis=0)
        heads = nn(head[...], hot).astype(BF16)
        in_row, in_col = window(row, r_at), window(col, c_at) * conf
        in_col = jnp.concatenate([in_col, in_col], axis=0)
        lefts = [heads * in_row[i : i + 1, :] for i in range(rows)]
        half = max(rows // 2, 4)
        sums = [nt(jnp.concatenate(lefts[i : i + half], axis=0), in_col) for i in range(0, rows, half)]
        sums = jnp.concatenate(sums, axis=0)
        sums = [jnp.where(left, sums[i : i + 32], sums[i + 32 : i + 64]) for i in range(0, 32 * rows, 64)]
        return jnp.concatenate(sums, axis=0)

    total = factors(own, 16)
    total = jnp.concatenate([total[:64] + factors(below, 4), total[64:]], axis=0)
    total = total * 0.25

    sub = iota((8, 128), 0)
    mine = (sub >> 2) == (iota((8, 128), 1) >> 6)
    blocks = []
    for j in range(8):
        cells = slice(j * 128, (j + 1) * 128)
        h = total[j * 32 : (j + 1) * 32, :]
        terms = [up[k * 16 : (k + 1) * 16, cells].astype(F32) * h[k : k + 1, :] for k in range(C2)]
        while len(terms) > 1:
            terms = [a + b for a, b in zip(terms[0::2], terms[1::2])]
        pieces = []
        for v in (terms[0][:8], terms[0][8:]):
            turned = pltpu.roll(v, 4, 0)
            pieces.append(jnp.where(mine, jnp.where(sub < 4, v, turned), 0.0))
            pieces.append(jnp.where(mine, jnp.where(sub < 4, turned, v), 0.0))
        blocks.append(jnp.concatenate(pieces, axis=1))
    flat = jnp.concatenate(blocks, axis=0)
    top = flat.astype(BF16)
    rest = (flat - top.astype(F32)).astype(BF16)
    both = nn(jnp.concatenate([top, rest], axis=0), spread[...])
    out[...] = both[:64] + both[64:]


def on_device(
    embedding,
    prompt_tile,
    crop_row,
    crop_col,
    points,
    confidence,
    pe_matrix,
    point_embed,
    w_one,
    w_two,
    w_three,
    conv_one,
    conv_two,
):
    vmem = pl.BlockSpec(memory_space=pltpu.VMEM)
    hbm = pl.BlockSpec(memory_space=pl.ANY)
    weights = (
        embedding.reshape(CELLS, C),
        conv_one,
        conv_two,
        pe_matrix,
        point_embed.reshape(1, 256),
        w_one,
        w_two,
        w_three.T,
    )
    up_shape = pltpu.VMEM((16 * C2, CELLS), BF16)
    head_shape = pltpu.VMEM((C2, 256), BF16)
    tables = (up_shape, head_shape, pltpu.VMEM((512, 256), BF16))
    scratch = [pltpu.VMEM(w.shape, w.dtype) for w in weights] + [pltpu.SemaphoreType.DMA((8,))]
    send, *made = pl.pallas_call(
        slots_kernel,
        out_shape=(pltpu.VMEM((NZ * NC, 1, 128), F32), *tables),
        in_specs=[vmem] * 5 + [hbm] * 8,
        out_specs=(vmem,) * 4,
        scratch_shapes=scratch,
    )(
        prompt_tile.reshape(1, P_DEV),
        crop_row.reshape(1, P_DEV),
        crop_col.reshape(1, P_DEV),
        points.T,
        confidence.reshape(1, P_DEV),
        *weights,
    )
    got = exchanged(send, column_groups())
    send, *made = pl.pallas_call(
        regroup_kernel,
        out_shape=(pltpu.VMEM((NX * NR, 8, 128), BF16), *tables),
        in_specs=[vmem] * 4 + [hbm] * 8,
        out_specs=(vmem,) * 4,
        scratch_shapes=scratch,
        input_output_aliases={1: 1, 2: 2, 3: 3},
    )(in_vmem(got), *map(in_vmem, made), *weights)
    got = exchanged(send, plane_groups())
    return pl.pallas_call(
        mask_kernel,
        out_shape=jax.ShapeDtypeStruct((4 * ROWS_T, 4 * EW), F32),
        in_specs=[vmem] * 4,
        out_specs=vmem,
    )(in_vmem(got), *map(in_vmem, made))


def solution(mesh):
    split = Mesh(mesh.devices.reshape(NX, NZ, NC, NR), EVERY)
    tile, every = EVERY[:3], EVERY
    return jax.shard_map(
        on_device,
        mesh=split,
        in_specs=(
            P(tile, None, None),
            P(every, None),
            P(every),
            P(every),
            P(every, None),
            P(every),
            P(),
            P(),
            P(),
            P(),
            P(),
            P(),
            P(),
        ),
        out_specs=P(tile, None),
        check_vma=False,
    )
```

```python
import math

import jax
import jax.numpy as jnp
from jax import lax
from jax.experimental import pallas as pl
from jax.experimental.pallas import tpu as pltpu
from jax.sharding import Mesh
from jax.sharding import PartitionSpec as P

CK = 4
C = 256
C1 = 64
C2 = 32
ROWS_T = 16
EW = 64
P_DEV = 128
NX, NZ, NC, NR = 4, 16, 2, 4
CELLS = ROWS_T * EW
Z_FIRST, C_FIRST, X_FIRST, R_FIRST = 11, 1, 2, 2
UNROLL, BLOCK = 4, 256
EVERY = ("x", "z", "core", "rep")
F32 = jnp.float32
BF16 = jnp.bfloat16
I32 = jnp.int32


def iota(shape, dim):
    return lax.broadcasted_iota(I32, shape, dim)


def flat(x, z, c, r):
    return ((x % NX * NZ + z % NZ) * NC + c % NC) * NR + r % NR


def exchanged(value, groups):
    return lax.all_to_all(value, EVERY, 0, 0, axis_index_groups=groups, tiled=True)


def column_groups():
    return [
        [flat(x, Z_FIRST + i, C_FIRST + j, r) for i in range(NZ) for j in range(NC)]
        for x in range(NX)
        for r in range(NR)
    ]


def plane_groups():
    return [
        [flat(X_FIRST + i, z, c, R_FIRST + j) for i in range(NX) for j in range(NR)]
        for z in range(NZ)
        for c in range(NC)
    ]


def nt(a, b):
    return lax.dot_general(a, b, (((1,), (1,)), ((), ())), preferred_element_type=F32)


def nn(a, b):
    return jnp.dot(a, b, preferred_element_type=F32)


def gelu(v):
    return 0.5 * v * (1.0 + lax.erf(v * (1.0 / math.sqrt(2.0))))


def local_tables(emb, one, two, pe, bias, w1, w2, w3, up_ref, head_ref, spread_ref):
    coord = (iota((16, P_DEV), 0).astype(F32) + 0.5) / (4.0 * CK) * 2.0 - 1.0
    angle_a = coord * pe[0:1, :] * (2.0 * math.pi)
    angle_b = coord * pe[1:2, :] * (2.0 * math.pi)
    sin_a, cos_a, sin_b, cos_b = jnp.sin(angle_a), jnp.cos(angle_a), jnp.sin(angle_b), jnp.cos(angle_b)
    sines, cosines = [], []
    for i in range(16):
        sin_i, cos_i = sin_a[i : i + 1, :], cos_a[i : i + 1, :]
        sines.append(sin_i * cos_b + cos_i * sin_b)
        cosines.append(cos_i * cos_b - sin_i * sin_b)
    sines, cosines = jnp.concatenate(sines, axis=0), jnp.concatenate(cosines, axis=0)
    tokens = (jnp.concatenate([sines, cosines], axis=1) + bias[...]).astype(BF16)
    hidden = jnp.maximum(nn(tokens, w1[...]), 0.0).astype(BF16)
    hidden = jnp.maximum(nn(hidden, w2[...]), 0.0).astype(BF16)
    head_ref[...] = nt(w3[...], hidden).astype(BF16)

    row = iota((16, P_DEV), 0)
    x, y = row >> 2, row & 3
    ahead = iota((16, P_DEV), 1) - (2 * (y & 1) + (x & 1)) * C2
    pick = jnp.concatenate([(ahead == k).astype(F32) for k in range(C2)], axis=0).astype(BF16)
    row = iota((16, 256), 0)
    keep = (iota((16, 256), 1) >> 6) == 2 * ((row & 3) >> 1) + (row >> 3)
    spread = nt(pick, jnp.concatenate([two[...]] * 4, axis=0))
    wide = [jnp.where(keep, spread[16 * k : 16 * k + 16], 0.0) for k in range(C2)]
    wide = jnp.concatenate(wide, axis=0).astype(BF16)
    one_t = one[...].astype(F32).T.astype(BF16)

    def block(i, carry):
        start = pl.multiple_of(i * BLOCK, BLOCK)
        first_up = nt(one_t, emb[pl.ds(start, BLOCK), :])
        parts = []
        for o in range(4):
            v = first_up[o * C1 : (o + 1) * C1, :]
            v = v - jnp.mean(v, axis=0, keepdims=True)
            v = v * lax.rsqrt(jnp.mean(v * v, axis=0, keepdims=True) + 1e-06)
            parts.append(gelu(v).astype(BF16))
        active = jnp.concatenate(parts, axis=0)
        up_ref[:, pl.ds(start, BLOCK)] = gelu(nn(wide, active)).astype(BF16)
        return carry

    ahead = iota((EW, 256), 1) - 4 * iota((EW, 256), 0)
    for x in range(4):
        lanes = (ahead == x).astype(F32).astype(BF16)
        spread_ref[x * 128 : x * 128 + 64, :] = lanes
        spread_ref[x * 128 + 64 : x * 128 + 128, :] = lanes
    lax.fori_loop(0, CELLS // BLOCK, block, 0, unroll=UNROLL)


def gathered_in(refs, bufs, sems):
    copies = [pltpu.make_async_copy(r, b, sems.at[i]) for i, (r, b) in enumerate(zip(refs, bufs))]
    for c in copies:
        c.start()
    for c in copies:
        c.wait()


def in_vmem(value):
    return pltpu.with_memory_space_constraint(value, pltpu.VMEM)


def is_early():
    return lax.axis_index("z") <= 5


def slots_kernel(tile, row, col, pts, conf, *rest):
    weights, (send, *tables), scratch = rest[:8], rest[8:12], rest[12:]
    bufs, sems = scratch[:8], scratch[8]
    t = tile[...]
    names = (iota((P_DEV, P_DEV), 0) == t).astype(F32)
    before = (iota((P_DEV, P_DEV), 0) < iota((P_DEV, P_DEV), 1)).astype(BF16)
    count = nn(names.astype(BF16), before)
    rank = jnp.sum(names * count, axis=0, keepdims=True).astype(I32)
    values = [row[...], col[...], conf[...], pts[0:1, :], pts[1:2, :]]
    group = iota((16, P_DEV), 0)
    x_of, s_of = group >> 2, group & 3
    dest = iota((NZ * NC, P_DEV), 0)

    def part(target, rank_at, values):
        mask = ((target >> 5) == x_of) & (rank_at == s_of)
        rows = [jnp.where(mask, v.astype(F32), 0.0) for v in values]
        rows += [jnp.zeros((16, P_DEV), F32)] * 3
        z, c = (target >> 1) - Z_FIRST, target - C_FIRST
        place = 2 * (z & 15) + (c & 1)
        return nt((place == dest).astype(BF16), jnp.concatenate(rows, axis=0).astype(BF16))

    out = part(t, rank, values) + part(t + 1, rank + 2, [values[0] - ROWS_T] + values[1:])
    send[...] = out.reshape(NZ * NC, 1, 128)

    @pl.when(is_early())
    def _():
        gathered_in(weights, bufs, sems)
        local_tables(*bufs, *tables)


def regroup_kernel(got, up_in, head_in, spread_in, *rest):
    weights, (send, *tables), scratch = rest[:8], rest[8:12], rest[12:]
    bufs, sems = scratch[:8], scratch[8]
    r = got[...].reshape(NZ * NC, 128)
    r = jnp.concatenate([r] * 4, axis=0)
    keep = (iota((128, 128), 1) & 3) == (iota((128, 128), 0) >> 5)
    r = jnp.where(keep, r, 0.0).astype(BF16)
    at, lane = iota((32, 128), 0), iota((32, 128), 1)
    pick = ((lane >> 4) == (at & 7)) & (((lane >> 2) & 3) == (at >> 3))
    out = nt(pick.astype(BF16), r)
    for i in range(NX):
        x = (X_FIRST + i) % NX
        for j in range(NR):
            send[i * NR + j] = out[x * 8 : (x + 1) * 8, :].astype(BF16)

    @pl.when(jnp.logical_not(is_early()))
    def _():
        gathered_in(weights, bufs, sems)
        local_tables(*bufs, *tables)


def mask_kernel(got, up, head, spread, out):
    lane = iota((8, 128), 1)
    own, below = [], []
    for j in range(8):
        a, b = got[j].astype(F32), got[j + 8].astype(F32)
        own.append(jnp.where(lane < 64, a, pltpu.roll(b, 64, 1)))
        below.append(jnp.where(lane < 64, pltpu.roll(a, 64, 1), b))
    own, below = (jnp.concatenate(v, axis=1).astype(BF16) for v in (own, below))
    many = 1024
    c_at = iota((EW, many), 0).astype(F32).astype(BF16)
    r_at = c_at[:16]
    zero, unit = BF16(0.0), BF16(1.0)
    left = iota((C2, 128), 1) < 64

    def window(v, at):
        return jnp.clip(BF16(2.5) - jnp.abs(at - (v + BF16(1.5))), zero, unit)

    def factors(v, rows):
        row, col, conf, first, second = (v[i : i + 1, :] for i in range(5))
        ahead = r_at - (BF16(16.0) * first + second)
        hot = [jnp.where(ahead == BF16(-16.0 * i), unit, zero) for i in range(16)]
        hot = jnp.concatenate(hot, axis=0)
        heads = nn(head[...], hot).astype(BF16)
        in_row, in_col = window(row, r_at), window(col, c_at) * conf
        in_col = jnp.concatenate([in_col, in_col], axis=0)
        lefts = [heads * in_row[i : i + 1, :] for i in range(rows)]
        half = max(rows // 2, 4)
        sums = [nt(jnp.concatenate(lefts[i : i + half], axis=0), in_col) for i in range(0, rows, half)]
        sums = jnp.concatenate(sums, axis=0)
        sums = [jnp.where(left, sums[i : i + 32], sums[i + 32 : i + 64]) for i in range(0, 32 * rows, 64)]
        return jnp.concatenate(sums, axis=0)

    total = factors(own, 16)
    total = jnp.concatenate([total[:64] + factors(below, 4), total[64:]], axis=0)
    total = total * 0.25

    sub = iota((8, 128), 0)
    mine = (sub >> 2) == (iota((8, 128), 1) >> 6)
    blocks = []
    for j in range(8):
        cells = slice(j * 128, (j + 1) * 128)
        h = total[j * 32 : (j + 1) * 32, :]
        terms = [up[k * 16 : (k + 1) * 16, cells].astype(F32) * h[k : k + 1, :] for k in range(C2)]
        while len(terms) > 1:
            terms = [a + b for a, b in zip(terms[0::2], terms[1::2])]
        pieces = []
        for v in (terms[0][:8], terms[0][8:]):
            turned = pltpu.roll(v, 4, 0)
            pieces.append(jnp.where(mine, jnp.where(sub < 4, v, turned), 0.0))
            pieces.append(jnp.where(mine, jnp.where(sub < 4, turned, v), 0.0))
        blocks.append(jnp.concatenate(pieces, axis=1))
    flat = jnp.concatenate(blocks, axis=0)
    top = flat.astype(BF16)
    rest = (flat - top.astype(F32)).astype(BF16)
    both = nn(jnp.concatenate([top, rest], axis=0), spread[...])
    out[...] = both[:64] + both[64:]


def on_device(
    embedding,
    prompt_tile,
    crop_row,
    crop_col,
    points,
    confidence,
    pe_matrix,
    point_embed,
    w_one,
    w_two,
    w_three,
    conv_one,
    conv_two,
):
    vmem = pl.BlockSpec(memory_space=pltpu.VMEM)
    hbm = pl.BlockSpec(memory_space=pl.ANY)
    weights = (
        embedding.reshape(CELLS, C),
        conv_one,
        conv_two,
        pe_matrix,
        point_embed.reshape(1, 256),
        w_one,
        w_two,
        w_three.T,
    )
    up_shape = pltpu.VMEM((16 * C2, CELLS), BF16)
    head_shape = pltpu.VMEM((C2, 256), BF16)
    tables = (up_shape, head_shape, pltpu.VMEM((512, 256), BF16))
    scratch = [pltpu.VMEM(w.shape, w.dtype) for w in weights] + [pltpu.SemaphoreType.DMA((8,))]
    send, *made = pl.pallas_call(
        slots_kernel,
        out_shape=(pltpu.VMEM((NZ * NC, 1, 128), F32), *tables),
        in_specs=[vmem] * 5 + [hbm] * 8,
        out_specs=(vmem,) * 4,
        scratch_shapes=scratch,
    )(
        prompt_tile.reshape(1, P_DEV),
        crop_row.reshape(1, P_DEV),
        crop_col.reshape(1, P_DEV),
        points.T,
        confidence.reshape(1, P_DEV),
        *weights,
    )
    got = exchanged(send, column_groups())
    send, *made = pl.pallas_call(
        regroup_kernel,
        out_shape=(pltpu.VMEM((NX * NR, 8, 128), BF16), *tables),
        in_specs=[vmem] * 4 + [hbm] * 8,
        out_specs=(vmem,) * 4,
        scratch_shapes=scratch,
        input_output_aliases={1: 1, 2: 2, 3: 3},
    )(in_vmem(got), *map(in_vmem, made), *weights)
    got = exchanged(send, plane_groups())
    return pl.pallas_call(
        mask_kernel,
        out_shape=jax.ShapeDtypeStruct((4 * ROWS_T, 4 * EW), F32),
        in_specs=[vmem] * 4,
        out_specs=vmem,
    )(in_vmem(got), *map(in_vmem, made))


def solution(mesh):
    split = Mesh(mesh.devices.reshape(NX, NZ, NC, NR), EVERY)
    tile, every = EVERY[:3], EVERY
    return jax.shard_map(
        on_device,
        mesh=split,
        in_specs=(
            P(tile, None, None),
            P(every, None),
            P(every),
            P(every),
            P(every, None),
            P(every),
            P(),
            P(),
            P(),
            P(),
            P(),
            P(),
            P(),
        ),
        out_specs=P(tile, None),
        check_vma=False,
    )
```
